32 devices in a mesh: dp: 4 (over z), ctx: 2 (over x), tensor: 4 (over y, core).
Axes of the slice: x: 2, y: 2, z: 4, core: 2. Of those that a mesh axis runs over, the one named last changes fastest.
Arguments:
- hidden_in: bfloat16 [4, 1024, 768], P('dp', ('ctx', 'tensor')), may hold values from -6 to 6
- cotangent: bfloat16 [4, 1024, 768], P('dp', ('ctx', 'tensor')), may hold values from -6 to 6
- segment_ids: int32 [4, 1024], P('dp'), may hold values from 0 to 3, never falling along the last dimension, each value on 1 to 512 neighbouring positions
- attend_gain: bfloat16 [768], P('dp'), may hold values from 0.099609375 to 1.8984375
- attend_shift: bfloat16 [768], P('dp'), may hold values from -3 to 3
- feed_gain: bfloat16 [768], P('dp'), may hold values from 0.099609375 to 1.8984375
- feed_shift: bfloat16 [768], P('dp'), may hold values from -3 to 3
- project_weight: bfloat16 [768, 3, 768], P('dp', None, 'tensor'), may hold values from -4 to 4
- project_bias: bfloat16 [3, 12, 64], P(None, 'tensor', 'dp'), may hold values from -3 to 3
- output_weight: bfloat16 [768, 768], P('tensor', 'dp'), may hold values from -0.875 to 0.875
- output_bias: bfloat16 [768], P('dp'), may hold values from -3 to 3
- upward_weight: bfloat16 [768, 3072], P('dp', 'tensor'), may hold values from -0.21875 to 0.21875
- upward_bias: bfloat16 [4, 768], P('tensor', 'dp'), may hold values from -3 to 3
- downward_weight: bfloat16 [3072, 768], P('tensor', 'dp'), may hold values from -0.109375 to 0.109375
- downward_bias: bfloat16 [768], P('dp'), may hold values from -3 to 3
Outputs:
- hidden_out: bfloat16 [4, 1024, 768], P('dp', ('ctx', 'tensor'))
- hidden_grad: bfloat16 [4, 1024, 768], P('dp', ('ctx', 'tensor'))
- attend_gain_grad: float32 [768], P('dp')
- attend_shift_grad: float32 [768], P('dp')
- feed_gain_grad: float32 [768], P('dp')
- feed_shift_grad: float32 [768], P('dp')
- project_weight_grad: float32 [768, 3, 768], P('dp', None, 'tensor')
- project_bias_grad: float32 [3, 12, 64], P(None, 'tensor', 'dp')
- output_weight_grad: float32 [768, 768], P('tensor', 'dp')
- output_bias_grad: float32 [768], P('dp')
- upward_weight_grad: float32 [768, 3072], P('dp', 'tensor')
- upward_bias_grad: float32 [4, 768], P('tensor', 'dp')
- downward_weight_grad: float32 [3072, 768], P('tensor', 'dp')
- downward_bias_grad: float32 [768], P('dp')
The draws below stay inside these ranges and needn't reach their ends.
Inputs may be any that keep to these rules, and one draw needn't show every extreme that they name: `segment_ids`: along each sequence the ids never fall; each of the 4 documents spans 1 to 512 tokens and one spans exactly 512.
All inputs are finite; a program needn't handle non-finite values.
Results may differ from the reference program's by a relative error of at most 0.013.
Values may be sent and summed in bfloat16 or wider, within the bound.
No kernel may reach another device: no remote copies, remote signals or barrier semaphores. Data moves between devices by JAX's collectives and lax.ppermute only.
A program may use at most 64 MiB of HBM per device.

```python
import math
import jax
import jax.numpy as jnp
import numpy as np
from jax import lax

D = 768
H = 12
HD = 64
ROT = 16
FF = 3072
LEN = 1024
DOCS = 4
NSEQ = 4
DOC_MAX = 512
FF_DEV = 768
N_TENSOR = 4


def draw_project_weight(key, part):
    base = jnp.clip(jax.random.normal(key, (D, 3, D), jnp.float32), -4.0, 4.0) * D ** (-0.5)
    return base.astype(jnp.bfloat16)


def block_levels(rng, extent, cuts, smallest, top_value):
    def one(position, blocks):
        draws = jax.random.uniform(jax.random.fold_in(jax.random.fold_in(rng, 6), position), (blocks,), jnp.float32, smallest / len(cuts), top_value / len(cuts))
        return jnp.repeat(jnp.exp(draws), extent[position] // blocks).reshape((-1,) + (1,) * (len(extent) - position - 1))

    loudness = one(*cuts[0])
    for cut in cuts[1:]:
        loudness = loudness * one(*cut)
    return loudness


def profile(amount, total, bound, lean):
    loads = [(1 << 20) // math.isqrt(rank ** lean) + 1 for rank in range(2, amount + 1)]
    rest, counts = total - bound - (amount - 1), [1] * (amount - 1)
    while rest > 0:
        candidates = [i for i in range(amount - 1) if counts[i] < bound]
        whole, left = sum([loads[i] for i in candidates]), rest
        for i in candidates:
            extra = min(bound - counts[i], max(1, left * loads[i] // whole), rest)
            counts[i] = counts[i] + extra
            rest = rest - extra
    return np.array([bound] + counts)


def ragged(rng, count, total, bound, skew):
    if count == 2:
        one = jax.random.randint(rng, (), max(1, total - bound), min(bound, total - 1) + 1)
        return jnp.stack([one, total - one])
    tallies = jnp.asarray(profile(count, total, bound, skew), jnp.int32)
    twos = (count - 1) // 2
    source_of, receiver = tallies[1:1 + 2 * twos:2], tallies[2:2 + 2 * twos:2]
    slack = jnp.minimum(source_of - 1, bound - receiver)
    shifted = jax.random.randint(jax.random.fold_in(rng, 1), (twos,), 0, 1 << 20) % (slack + 1)
    tallies = tallies.at[1:1 + 2 * twos:2].set(source_of - shifted).at[2:2 + 2 * twos:2].set(receiver + shifted)
    return tallies[jax.random.permutation(jax.random.fold_in(rng, 2), count)]


def gaussian(stream_key, shape, scale, limit, split=(), held_as=jnp.bfloat16):
    values = scale * jax.random.normal(stream_key, shape, jnp.float32)
    if split:
        values = values * block_levels(stream_key, shape, split, -0.22, 0.18)
    return jnp.clip(values, -limit, limit).astype(held_as)


def setup_inputs(seed: int = 0) -> dict:
    splits = jax.random.split(jax.random.key(seed), 16)
    hidden_in = gaussian(splits[0], (NSEQ, LEN, D), 1.0, 6.0, ((0, 4), (1, 8)))
    cotangent = gaussian(splits[1], (NSEQ, LEN, D), 1.0, 6.0, ((0, 4), (1, 8)))
    segment_ids = jax.vmap(lambda own: jnp.searchsorted(jnp.cumsum(ragged(own, DOCS, LEN, DOC_MAX, 0)), jnp.arange(LEN), side="right"))(jax.random.split(splits[2], NSEQ)).reshape((NSEQ, LEN)).astype(jnp.int32)
    attend_gain = jnp.clip(1.0 + 0.18 * jax.random.normal(splits[3], (D,), jnp.float32), 0.099609375, 1.8984375).astype(jnp.bfloat16)
    attend_shift = gaussian(splits[4], (D,), 0.5, 3.0, ((0, 4),))
    feed_gain = jnp.clip(1.0 + 0.18 * jax.random.normal(splits[5], (D,), jnp.float32), 0.099609375, 1.8984375).astype(jnp.bfloat16)
    feed_shift = gaussian(splits[6], (D,), 0.5, 3.0, ((0, 4),))
    project_weight = draw_project_weight(jax.random.fold_in(splits[15], 71), 0)
    project_bias = gaussian(splits[8], (3, H, HD), 0.5, 3.0, ((1, 4), (2, 4)))
    output_weight = gaussian(splits[9], (D, D), (D // 16) ** -0.5, 0.875, ((0, 4), (1, 4)))
    output_bias = gaussian(splits[10], (D,), 0.5, 3.0, ((0, 4),))
    upward_weight = gaussian(splits[11], (D, FF), D ** -0.5, 0.21875, ((0, 4), (1, 4)))
    upward_bias = gaussian(splits[12], (N_TENSOR, FF_DEV), 0.5, 3.0, ((0, 4), (1, 4)))
    downward_weight = gaussian(splits[13], (FF, D), FF ** -0.5, 0.109375, ((0, 4), (1, 4)))
    downward_bias = gaussian(splits[14], (D,), 0.5, 3.0, ((0, 4),))
    return {"hidden_in": hidden_in, "cotangent": cotangent, "segment_ids": segment_ids, "attend_gain": attend_gain, "attend_shift": attend_shift, "feed_gain": feed_gain, "feed_shift": feed_shift, "project_weight": project_weight, "project_bias": project_bias, "output_weight": output_weight, "output_bias": output_bias, "upward_weight": upward_weight, "upward_bias": upward_bias, "downward_weight": downward_weight, "downward_bias": downward_bias}


epsilon = 1e-05
masked_score = -1e+30

def normalize(values):
    average = lax.optimization_barrier(jnp.mean(values, axis=-1, keepdims=True))
    centred = values - average
    variance = lax.optimization_barrier(jnp.mean(centred * centred, axis=-1, keepdims=True))
    inverse = lax.rsqrt(variance + epsilon)
    return (centred * inverse, inverse)

def rotary_tables(positions):
    half_rot = ROT // 2
    frequency = 10000.0 ** (-2.0 * jnp.arange(half_rot, dtype=jnp.float32) / ROT)
    angles = positions.astype(jnp.float32)[:, None] * frequency[None, :]
    return (jnp.cos(angles), jnp.sin(angles))

def rotate(tensor, cosine, sine_table, direction):
    half_rot = ROT // 2
    first_half = tensor[..., :half_rot]
    second_half = tensor[..., half_rot:ROT]
    cosine_wide = cosine[:, None, :]
    sine_wide = direction * sine_table[:, None, :]
    return jnp.concatenate([first_half * cosine_wide - second_half * sine_wide, second_half * cosine_wide + first_half * sine_wide, tensor[..., ROT:]], axis=-1)

def gelu_pair(preact):
    cumulative = 0.5 * (1.0 + jax.scipy.special.erf(preact * 0.7071067811865476))
    density = jnp.exp(-0.5 * preact * preact) * 0.3989422804014327
    return (preact * cumulative, cumulative + preact * density)

def reference(hidden_in, cotangent, segment_ids, attend_gain, attend_shift, feed_gain, feed_shift, project_weight, project_bias, output_weight, output_bias, upward_weight, upward_bias, downward_weight, downward_bias):
    score_scale = 1.0 / math.sqrt(HD)
    positions = jnp.arange(LEN, dtype=jnp.int32)
    cosine, sine_table = rotary_tables(positions)
    causal = positions[None, :] <= positions[:, None]
    gain_first = attend_gain.astype(jnp.float32)
    shift_first = attend_shift.astype(jnp.float32)
    gain_second = feed_gain.astype(jnp.float32)
    shift_second = feed_shift.astype(jnp.float32)
    weight_flat = project_weight.reshape(D, 3 * D)
    bias_query = project_bias[0].astype(jnp.float32)
    bias_key = project_bias[1].astype(jnp.float32)
    bias_value = project_bias[2].astype(jnp.float32)
    upward_flat = upward_bias.reshape(FF).astype(jnp.float32)
    bias_sum = output_bias.astype(jnp.float32) + downward_bias.astype(jnp.float32)

    def sequence_step(running, inputs):
        tokens, grad_out, segments = inputs
        source = tokens.astype(jnp.float32)
        normed, inverse = normalize(source)
        first_in = (normed * gain_first + shift_first).astype(jnp.bfloat16)
        second_in = (normed * gain_second + shift_second).astype(jnp.bfloat16)
        projected = jnp.dot(first_in, weight_flat, preferred_element_type=jnp.float32).reshape(LEN, 3, H, HD)
        queries = rotate(projected[:, 0] + bias_query, cosine, sine_table, 1.0).astype(jnp.bfloat16)
        keys_all = rotate(projected[:, 1] + bias_key, cosine, sine_table, 1.0).astype(jnp.bfloat16)
        values_all = (projected[:, 2] + bias_value).astype(jnp.bfloat16)
        allowed = causal & (segments[:, None] == segments[None, :])
        scores = jnp.einsum('qhd,khd->hqk', queries.astype(jnp.float32), keys_all.astype(jnp.float32)) * score_scale
        scores = jnp.where(allowed[None], scores, masked_score)
        highest = lax.optimization_barrier(jnp.max(scores, axis=-1, keepdims=True))
        exponent = jnp.exp(scores - highest)
        row_sum = lax.optimization_barrier(jnp.sum(exponent, axis=-1, keepdims=True))
        log_total = highest + jnp.log(row_sum)
        weights = (exponent / row_sum).astype(jnp.bfloat16)
        attended = jnp.einsum('hqk,khd->qhd', weights.astype(jnp.float32), values_all.astype(jnp.float32)).astype(jnp.bfloat16)
        attended_flat = attended.reshape(LEN, D)
        preact = jnp.dot(second_in, upward_weight, preferred_element_type=jnp.float32) + upward_flat
        activated, slope = gelu_pair(preact)
        hidden_act = activated.astype(jnp.bfloat16)
        mixed = jnp.dot(attended_flat, output_weight, preferred_element_type=jnp.float32) + jnp.dot(hidden_act, downward_weight, preferred_element_type=jnp.float32)
        result = (source + mixed + bias_sum).astype(jnp.bfloat16)
        grad_float = grad_out.astype(jnp.float32)
        bias_grad = lax.optimization_barrier(jnp.sum(grad_float, axis=0))
        grad_down = jnp.dot(hidden_act.T, grad_out, preferred_element_type=jnp.float32)
        grad_outw = jnp.dot(attended_flat.T, grad_out, preferred_element_type=jnp.float32)
        grad_pre = jnp.dot(grad_out, downward_weight.T, preferred_element_type=jnp.float32) * slope
        grad_pre_b = grad_pre.astype(jnp.bfloat16)
        grad_up = jnp.dot(second_in.T, grad_pre_b, preferred_element_type=jnp.float32)
        grad_upbias = lax.optimization_barrier(jnp.sum(grad_pre, axis=0))
        grad_second = jnp.dot(grad_pre_b, upward_weight.T, preferred_element_type=jnp.float32)
        grad_att = jnp.dot(grad_out, output_weight.T, preferred_element_type=jnp.float32).astype(jnp.bfloat16).reshape(LEN, H, HD)
        probabilities = jnp.exp(scores - log_total)
        probs_b = probabilities.astype(jnp.bfloat16)
        grad_values = jnp.einsum('hqk,qhd->khd', probs_b.astype(jnp.float32), grad_att.astype(jnp.float32))
        grad_probs = jnp.einsum('qhd,khd->hqk', grad_att.astype(jnp.float32), values_all.astype(jnp.float32))
        row_delta = lax.optimization_barrier(jnp.sum(grad_att.astype(jnp.float32) * attended.astype(jnp.float32), axis=-1)).T[:, :, None]
        grad_scores = (probabilities * (grad_probs - row_delta)).astype(jnp.bfloat16)
        grad_queries = jnp.einsum('hqk,khd->qhd', grad_scores.astype(jnp.float32), keys_all.astype(jnp.float32)) * score_scale
        grad_keys = jnp.einsum('hqk,qhd->khd', grad_scores.astype(jnp.float32), queries.astype(jnp.float32)) * score_scale
        grad_queries = rotate(grad_queries, cosine, sine_table, -1.0)
        grad_keys = rotate(grad_keys, cosine, sine_table, -1.0)
        grad_proj = jnp.stack([grad_queries, grad_keys, grad_values], axis=1).astype(jnp.bfloat16).reshape(LEN, 3 * D)
        grad_pbias = jnp.stack([lax.optimization_barrier(jnp.sum(grad_queries, axis=0)), lax.optimization_barrier(jnp.sum(grad_keys, axis=0)), lax.optimization_barrier(jnp.sum(grad_values, axis=0))])
        grad_project = jnp.dot(first_in.T, grad_proj, preferred_element_type=jnp.float32).reshape(D, 3, D)
        grad_first = jnp.dot(grad_proj, weight_flat.T, preferred_element_type=jnp.float32)
        grad_normed = grad_first * gain_first + grad_second * gain_second
        grad_inner = inverse * (grad_normed - lax.optimization_barrier(jnp.mean(grad_normed, axis=-1, keepdims=True)) - normed * lax.optimization_barrier(jnp.mean(grad_normed * normed, axis=-1, keepdims=True)))
        input_grad = (grad_float + grad_inner).astype(jnp.bfloat16)
        updates = (lax.optimization_barrier(jnp.sum(grad_first * normed, axis=0)), lax.optimization_barrier(jnp.sum(grad_first, axis=0)), lax.optimization_barrier(jnp.sum(grad_second * normed, axis=0)), lax.optimization_barrier(jnp.sum(grad_second, axis=0)), bias_grad, grad_project, grad_pbias, grad_outw, grad_up, grad_upbias, grad_down)
        running = jax.tree.map(jnp.add, running, updates)
        return (running, (result, input_grad))
    initial = (jnp.zeros((D,), jnp.float32), jnp.zeros((D,), jnp.float32), jnp.zeros((D,), jnp.float32), jnp.zeros((D,), jnp.float32), jnp.zeros((D,), jnp.float32), jnp.zeros((D, 3, D), jnp.float32), jnp.zeros((3, H, HD), jnp.float32), jnp.zeros((D, D), jnp.float32), jnp.zeros((D, FF), jnp.float32), jnp.zeros((FF,), jnp.float32), jnp.zeros((FF, D), jnp.float32))
    totals, stacked = lax.scan(sequence_step, initial, (hidden_in, cotangent, segment_ids))
    hidden_out, hidden_grad = stacked
    return (hidden_out, hidden_grad, totals[0], totals[1], totals[2], totals[3], totals[5], totals[6], totals[7], totals[4], totals[8], totals[9].reshape(N_TENSOR, FF // N_TENSOR), totals[10], totals[4])
```

```python
import jax
import jax.numpy as jnp
from jax import lax
from jax.experimental import pallas as pl
from jax.experimental.pallas import tpu as pltpu
from jax.sharding import PartitionSpec as P

HD = 64
ROT = 16
HALF = ROT // 2
DOC_MAX = 512
ROWS = 256

epsilon = 1e-05
masked_score = -1e30
f32 = jnp.float32
bf16 = jnp.bfloat16


def flipped(block, axis, bit):
    return lax.ppermute(block, axis, [(i, i ^ bit) for i in range(lax.axis_size(axis))])


def ordered(own, other, second, dim):
    return jnp.where(
        second, jnp.stack([other, own], axis=dim), jnp.stack([own, other], axis=dim)
    )


def gather_tokens(rows):
    block = rows
    dims = 0
    for axis in ("ctx", "tensor"):
        index = lax.axis_index(axis)
        bit = lax.axis_size(axis) // 2
        while bit:
            block = ordered(block, flipped(block, axis, bit), (index & bit) > 0, dims)
            bit //= 2
            dims += 1
    return block.reshape(-1, rows.shape[-1])


def gather_dp(block):
    count = lax.axis_size("dp")
    return lax.all_to_all(jnp.broadcast_to(block[None], (count,) + block.shape), "dp", 0, 0)


def scatter_rows(partial):
    count = lax.axis_size("ctx") * lax.axis_size("tensor")
    blocks = partial.reshape(count, partial.shape[0] // count, partial.shape[1])
    return lax.all_to_all(blocks, ("ctx", "tensor"), 0, 0)


def high_low(values):
    high = lax.reduce_precision(values, 8, 7)
    return jnp.stack([high, values - high]).astype(bf16)


def pad_rows(block, rows):
    return jnp.pad(block, ((0, rows - block.shape[0]), (0, 0)))


def gelu_pair(preact):
    cumulative = 0.5 * (1.0 + jax.scipy.special.erf(preact * 0.7071067811865476))
    density = jnp.exp(-0.5 * preact * preact) * 0.3989422804014327
    return (preact * cumulative, cumulative + preact * density)


def dot(left, right, dims):
    return lax.dot_general(left, right, (dims, ((), ())), preferred_element_type=f32)


def attention_kernel(
    qkv_ref, bias_ref, cos_ref, sin_ref, seg_row_ref, seg_col_ref, grad_ref,
    att_ref, grad_proj_ref, bias_grad_ref, dq_ref, dk_ref, dv_ref,
):
    width, tokens = grad_ref.shape
    cosine = cos_ref[...]
    sine = sin_ref[...]
    scale = HD**-0.5

    def rotate(block, direction):
        first, second = block[:HALF], block[HALF:ROT]
        return jnp.concatenate(
            [
                first * cosine - second * (direction * sine),
                second * cosine + first * (direction * sine),
                block[ROT:],
            ],
            axis=0,
        )

    def head(index, carry):
        start = pl.multiple_of(index * HD, HD)

        def rows(part):
            return pl.ds(part * width + start, HD)

        queries = rotate(qkv_ref[rows(0), :] + bias_ref[rows(0), :], 1.0).astype(bf16)
        keys = rotate(qkv_ref[rows(1), :] + bias_ref[rows(1), :], 1.0).astype(bf16)
        values = (qkv_ref[rows(2), :] + bias_ref[rows(2), :]).astype(bf16)
        queries = queries * jnp.asarray(scale, bf16)
        grads = grad_ref[pl.ds(start, HD), :]
        key_rows = keys.T
        value_rows = values.T
        dk_ref[...] = jnp.zeros(dk_ref.shape, f32)
        dv_ref[...] = jnp.zeros(dv_ref.shape, f32)
        for block in range(tokens // ROWS):
            begin, end = block * ROWS, (block + 1) * ROWS
            low = max(0, (begin - DOC_MAX + 1) // ROWS * ROWS)
            query = queries[:, begin:end]
            grad = grads[:, begin:end]
            scores = dot(key_rows[low:end], query, ((1,), (0,)))
            key_at = lax.broadcasted_iota(jnp.int32, scores.shape, 0) + low
            query_at = lax.broadcasted_iota(jnp.int32, scores.shape, 1) + begin
            allowed = (seg_col_ref[low:end, :] == seg_row_ref[:, begin:end]) & (
                key_at <= query_at
            )
            scores = jnp.where(allowed, scores, masked_score)
            highest = jnp.max(scores, axis=0, keepdims=True)
            exponent = jnp.exp(scores - highest)
            probs = exponent * (1.0 / jnp.sum(exponent, axis=0, keepdims=True))
            probs_b = probs.astype(bf16)
            attended = dot(values[:, low:end], probs_b, ((1,), (0,))).astype(bf16)
            att_ref[pl.ds(start, HD), begin:end] = attended
            delta = jnp.sum(
                grad.astype(f32) * attended.astype(f32), axis=0, keepdims=True
            )
            grad_probs = dot(value_rows[low:end], grad, ((1,), (0,)))
            grad_scores = (probs * (grad_probs - delta)).astype(bf16)
            dq_ref[:, begin:end] = dot(keys[:, low:end], grad_scores, ((1,), (0,))) * scale
            dk_ref[:, low:end] += dot(query, grad_scores, ((1,), (1,)))
            dv_ref[:, low:end] += dot(grad, probs_b, ((1,), (1,)))
        for part, result in enumerate(
            (rotate(dq_ref[...], -1.0), rotate(dk_ref[...], -1.0), dv_ref[...])
        ):
            grad_proj_ref[rows(part), :] = result.astype(bf16)
            bias_grad_ref[rows(part), :] = jnp.sum(result, axis=1, keepdims=True)
        return carry

    lax.fori_loop(0, width // HD, head, 0)


def attention(qkv, bias, cosine, sine, segments, grad):
    width, tokens = grad.shape
    whole = pl.BlockSpec(memory_space=pltpu.VMEM)
    pairs = tokens * (DOC_MAX + ROWS) * (width // HD)
    return pl.pallas_call(
        attention_kernel,
        out_shape=(
            jax.ShapeDtypeStruct((width, tokens), bf16),
            jax.ShapeDtypeStruct((3 * width, tokens), bf16),
            jax.ShapeDtypeStruct((3 * width, 1), f32),
        ),
        in_specs=[whole] * 7,
        out_specs=(whole, whole, whole),
        scratch_shapes=[pltpu.VMEM((HD, tokens), f32)] * 3,
        cost_estimate=pl.CostEstimate(
            flops=pairs * HD * 10, transcendentals=pairs, bytes_accessed=tokens * width * 24
        ),
        name="attention",
    )(qkv, bias, cosine, sine, segments[None, :], segments[:, None], grad)


def body(
    hidden_in, cotangent, segment_ids, attend_gain, attend_shift, feed_gain, feed_shift,
    project_weight, project_bias, output_weight, output_bias,
    upward_weight, upward_bias, downward_weight, downward_bias,
):
    n_dp, n_ctx, n_tensor = (lax.axis_size(a) for a in ("dp", "ctx", "tensor"))
    dp_index, ctx_index = lax.axis_index("dp"), lax.axis_index("ctx")
    second = ctx_index > 0
    share, _, width = project_weight.shape
    model = share * n_dp
    units = upward_weight.shape[1]
    half_units = units // n_ctx
    half_share = share // n_ctx
    heads = width // HD

    def own_half(block, size, axis):
        return lax.dynamic_slice_in_dim(block, ctx_index * size, size, axis)

    packed = jnp.concatenate(
        [
            own_half(project_weight, half_share, 0).reshape(half_share, 3 * width),
            own_half(output_weight, half_share, 1).T,
        ],
        axis=1,
    )
    small = jnp.concatenate(
        [
            attend_gain, attend_shift, feed_gain, feed_shift, output_bias, downward_bias,
            upward_bias[0], project_bias.reshape(-1),
        ]
    )
    columns = 4 * width
    small_rows = -(-small.shape[0] // (8 * columns)) * 8
    small_block = jnp.pad(small, (0, small_rows * columns - small.shape[0]))
    packed = jnp.concatenate([packed, small_block.reshape(small_rows, columns)], axis=0)
    attention_all = gather_dp(packed)
    feed_all = gather_dp(
        jnp.concatenate(
            [own_half(upward_weight, half_units, 1), own_half(downward_weight, half_units, 0).T],
            axis=0,
        )
    )
    hidden_rows = hidden_in[0]
    grad_rows = cotangent[0]
    hidden_all = gather_tokens(hidden_rows)
    grad_all = gather_tokens(grad_rows)
    tokens = hidden_all.shape[0]

    attention_half = attention_all[:, :half_share]
    weights = ordered(attention_half, flipped(attention_half, "ctx", 1), second, 1)
    weights = weights.reshape(model, columns)
    weight_project, weight_output = weights[:, : 3 * width], weights[:, 3 * width :]
    params = attention_all[:, half_share:].reshape(n_dp, -1)[:, : small.shape[0]].astype(f32)
    vectors = params[:, : 6 * share].reshape(n_dp, 6, share).transpose(1, 0, 2).reshape(6, model)
    gain_one, shift_one, gain_two, shift_two, bias_output, bias_downward = (
        vectors[i] for i in range(6)
    )
    unit_share = units // n_dp
    bias_upward = own_half(
        params[:, 6 * share : 6 * share + unit_share].reshape(units), half_units, 0
    )
    bias_project = (
        params[:, 6 * share + unit_share :]
        .reshape(n_dp, 3, heads, HD // n_dp)
        .transpose(1, 2, 0, 3)
        .reshape(3 * width, 1)
    )
    weight_up = feed_all[:, :share].reshape(model, half_units)
    weight_down = feed_all[:, share:].reshape(model, half_units)

    source = hidden_all.astype(f32)
    centred = source - jnp.mean(source, axis=-1, keepdims=True)
    inverse = lax.rsqrt(jnp.mean(centred * centred, axis=-1, keepdims=True) + epsilon)
    normed = centred * inverse
    first_in = (normed * gain_one + shift_one).astype(bf16)
    second_in = (normed * gain_two + shift_two).astype(bf16)

    frequency = 10000.0 ** (-2.0 * jnp.arange(HALF, dtype=f32) / ROT)
    angles = frequency[:, None] * jnp.arange(tokens, dtype=f32)[None, :]
    qkv = dot(weight_project, first_in, ((0,), (1,)))
    grad_att = dot(weight_output, grad_all, ((0,), (1,))).astype(bf16)
    attended, grad_proj, bias_grad = attention(
        qkv, bias_project, jnp.cos(angles), jnp.sin(angles), segment_ids[0], grad_att
    )

    grad_weights = jnp.concatenate(
        [dot(first_in, grad_proj, ((0,), (1,))), dot(grad_all, attended, ((0,), (1,)))], axis=1
    ).astype(bf16)
    grad_half = lax.dynamic_index_in_dim(
        grad_weights.reshape(n_dp, n_ctx, half_share, columns), ctx_index, 1, keepdims=False
    )
    bias_block = pad_rows(
        jnp.pad(high_low(bias_grad[:, 0]), ((0, 0), (0, columns - 3 * width))), 8
    )
    attention_parts = lax.all_to_all(
        jnp.concatenate(
            [grad_half, jnp.broadcast_to(bias_block[None], (n_dp, 8, columns))], axis=1
        ),
        "dp", 0, 0,
    )

    preact = dot(second_in, weight_up, ((1,), (0,))) + bias_upward
    activated, slope = gelu_pair(preact)
    hidden_act = activated.astype(bf16)
    grad_pre = dot(grad_all, weight_down, ((1,), (0,))) * slope
    grad_pre_b = grad_pre.astype(bf16)
    grad_feed = jnp.concatenate(
        [
            dot(second_in, grad_pre_b, ((0,), (0,))).reshape(n_dp, share, half_units),
            dot(grad_all, hidden_act, ((0,), (0,))).reshape(n_dp, share, half_units),
        ],
        axis=1,
    ).astype(bf16)
    unit_block = pad_rows(high_low(jnp.sum(grad_pre, axis=0)), 8)
    feed_parts = lax.all_to_all(
        jnp.concatenate(
            [grad_feed, jnp.broadcast_to(unit_block[None], (n_dp, 8, half_units))], axis=1
        ),
        "dp", 0, 0,
    )

    part = 1.0 / n_ctx
    mixed = dot(hidden_act, weight_down, ((1,), (1,))) + part * dot(
        attended, weight_output, ((0,), (1,))
    )
    mixed_parts = scatter_rows(mixed.astype(bf16))
    grad_first = part * dot(grad_proj, weight_project, ((0,), (1,)))
    grad_second = dot(grad_pre_b, weight_up, ((1,), (1,)))
    normed_parts = scatter_rows((grad_first * gain_one + grad_second * gain_two).astype(bf16))
    sums = jnp.stack(
        [
            jnp.sum(grad_first * normed, axis=0),
            jnp.sum(grad_first, axis=0),
            jnp.sum(grad_second * normed, axis=0),
            jnp.sum(grad_second, axis=0),
            jnp.sum(grad_rows.astype(f32), axis=0),
        ]
    )
    sums = sums.reshape(5, n_dp, share).transpose(1, 0, 2)
    sums = jnp.broadcast_to(sums[:, None], (n_dp, n_ctx * n_tensor, 5, share))
    sums = lax.all_to_all(
        sums.reshape(-1, 5, share), ("dp", "ctx", "tensor"), 0, 0
    ).sum(axis=0)

    own_source = hidden_rows.astype(f32)
    hidden_out = own_source + jnp.sum(mixed_parts.astype(f32), axis=0)
    hidden_out = (hidden_out + (bias_output + bias_downward)).astype(bf16)[None]

    own_centred = own_source - jnp.mean(own_source, axis=-1, keepdims=True)
    own_inverse = lax.rsqrt(jnp.mean(own_centred * own_centred, axis=-1, keepdims=True) + epsilon)
    own_normed = own_centred * own_inverse
    grad_normed = jnp.sum(normed_parts.astype(f32), axis=0)
    grad_inner = own_inverse * (
        grad_normed
        - jnp.mean(grad_normed, axis=-1, keepdims=True)
        - own_normed * jnp.mean(grad_normed * own_normed, axis=-1, keepdims=True)
    )
    hidden_grad = (grad_rows.astype(f32) + grad_inner).astype(bf16)[None]

    attention_sum = jnp.sum(attention_parts.astype(f32), axis=0)
    attention_own = lax.reduce_precision(attention_sum[:half_share], 8, 7).astype(bf16)
    attention_both = ordered(attention_own, flipped(attention_own, "ctx", 1), second, 0)
    attention_both = attention_both.reshape(share, columns).astype(f32)
    project_bias_sum = (attention_sum[half_share] + attention_sum[half_share + 1])[: 3 * width]
    bias_share = HD // n_dp
    project_bias_grad = lax.dynamic_slice_in_dim(
        project_bias_sum.reshape(3, heads, HD), dp_index * bias_share, bias_share, 2
    )

    feed_sum = jnp.sum(feed_parts.astype(f32), axis=0)
    unit_sum = feed_sum[2 * share] + feed_sum[2 * share + 1]
    feed_own = jnp.concatenate(
        [
            lax.reduce_precision(feed_sum[: 2 * share], 8, 7).astype(bf16),
            pad_rows(high_low(unit_sum), 8),
        ],
        axis=0,
    )
    feed_both = ordered(feed_own, flipped(feed_own, "ctx", 1), second, 0).astype(f32)
    upward_grad = feed_both[:, :share].transpose(1, 0, 2).reshape(share, units)
    downward_grad = feed_both[:, share : 2 * share].transpose(0, 2, 1).reshape(units, share)
    unit_both = (feed_both[:, 2 * share] + feed_both[:, 2 * share + 1]).reshape(units)
    upward_bias_grad = lax.dynamic_slice_in_dim(unit_both, dp_index * unit_share, unit_share)[None]

    return (
        hidden_out,
        hidden_grad,
        sums[0],
        sums[1],
        sums[2],
        sums[3],
        attention_both[:, : 3 * width].reshape(share, 3, width),
        project_bias_grad,
        attention_both[:, 3 * width :].T,
        sums[4],
        upward_grad,
        upward_bias_grad,
        downward_grad,
        sums[4],
    )


def solution(mesh):
    rows = P("dp", ("ctx", "tensor"), None)
    in_specs = (
        rows, rows, P("dp", None), P("dp"), P("dp"), P("dp"), P("dp"),
        P("dp", None, "tensor"), P(None, "tensor", "dp"), P("tensor", "dp"), P("dp"),
        P("dp", "tensor"), P("tensor", "dp"), P("tensor", "dp"), P("dp"),
    )
    out_specs = (
        rows, rows, P("dp"), P("dp"), P("dp"), P("dp"),
        P("dp", None, "tensor"), P(None, "tensor", "dp"), P("tensor", "dp"), P("dp"),
        P("dp", "tensor"), P("tensor", "dp"), P("tensor", "dp"), P("dp"),
    )
    return jax.shard_map(body, mesh=mesh, in_specs=in_specs, out_specs=out_specs, check_vma=False)
```

```python
import jax
import jax.numpy as jnp
from jax import lax
from jax.experimental import pallas as pl
from jax.experimental.pallas import tpu as pltpu
from jax.sharding import PartitionSpec as P

HD = 64
ROT = 16
HALF = ROT // 2
DOC_MAX = 512
ROWS = 256

epsilon = 1e-05
masked_score = -1e30
f32 = jnp.float32
bf16 = jnp.bfloat16


def flipped(block, axis, bit):
    return lax.ppermute(block, axis, [(i, i ^ bit) for i in range(lax.axis_size(axis))])


def ordered(own, other, second, dim):
    return jnp.where(
        second, jnp.stack([other, own], axis=dim), jnp.stack([own, other], axis=dim)
    )


def joined(own, other, second):
    return jnp.where(
        second, jnp.concatenate([other, own], axis=1), jnp.concatenate([own, other], axis=1)
    )


def gather_tokens(rows):
    block = rows
    dims = 0
    first = None
    for axis in ("ctx", "tensor"):
        index = lax.axis_index(axis)
        bit = lax.axis_size(axis) // 2
        while bit:
            other = flipped(block, axis, bit)
            first = other if first is None else first
            block = ordered(block, other, (index & bit) > 0, dims)
            bit //= 2
            dims += 1
    return block.reshape(-1, rows.shape[-1]), first


def gather_dp(block):
    count = lax.axis_size("dp")
    return lax.all_to_all(jnp.broadcast_to(block[None], (count,) + block.shape), "dp", 0, 0)


def exchange_dp(blocks):
    return lax.all_to_all(blocks, "dp", 0, 0)


def total_over(values, axes):
    for axis in axes:
        bit = 1
        while bit < lax.axis_size(axis):
            values = values + flipped(values, axis, bit)
            bit *= 2
    return values


def halve_rows(partial):
    rows = partial.astype(bf16)
    for axis in ("tensor", "ctx"):
        index, size, bit = lax.axis_index(axis), lax.axis_size(axis), 1
        outer = lax.axis_size("ctx") if axis == "tensor" else 1
        while bit < size:
            view = rows.reshape(outer * (size // bit // 2), 2, -1, rows.shape[-1])
            mine = (index // bit) % 2
            away = lax.dynamic_index_in_dim(view, 1 - mine, 1, keepdims=False)
            kept = lax.dynamic_index_in_dim(view, mine, 1, keepdims=False).astype(f32)
            rows = kept + flipped(away, axis, bit).astype(f32)
            last = axis == "ctx" and bit * 2 == size
            rows = rows.astype(f32 if last else bf16).reshape(-1, rows.shape[-1])
            bit *= 2
    return rows


def gelu_pair(preact):
    cumulative = 0.5 * (1.0 + jax.scipy.special.erf(preact * 0.7071067811865476))
    density = jnp.exp(-0.5 * preact * preact) * 0.3989422804014327
    return (preact * cumulative, cumulative + preact * density)


def dot(left, right, dims):
    return lax.dot_general(left, right, (dims, ((), ())), preferred_element_type=f32)


def attention_kernel(
    ctx_ref, all_ref, normed_ref, cot_ref, cos_ref, sin_ref, seg_row_ref, seg_col_ref,
    vectors_ref, mixed_ref, grad_normed_ref, grad_weights_ref, sums_ref, bias_grad_ref,
    weights_ref, first_ref, qkv_ref, grad_ref, feature_ref, dq_ref, dk_ref, dv_ref,
):
    tokens, model = normed_ref.shape
    shares, share = all_ref.shape[0], all_ref.shape[1] - 8
    width = grad_ref.shape[0]
    scale = HD**-0.5
    for s in range(shares):
        weights_ref[s * share : (s + 1) * share, :] = all_ref[s, :share, :]
    small = [all_ref[s, share:, :].astype(f32) for s in range(shares)]
    vectors = jnp.concatenate([piece[:, :share] for piece in small], axis=1)
    vectors_ref[...] = vectors
    bias = sum(piece[7:8, : 3 * width] for piece in small)
    gain, shift = vectors[0:1], vectors[1:2]
    project = weights_ref[:, : 3 * width]
    output = weights_ref[:, 3 * width :]
    chunks = [slice(i, i + ROWS) for i in range(0, tokens, ROWS)]
    for rows in chunks:
        first = (normed_ref[rows, :] * gain + shift).astype(bf16)
        first_ref[rows, :] = first
        qkv_ref[:, rows] = (dot(first, project, ((1,), (0,))) + bias).T
        grad_ref[:, rows] = dot(cot_ref[rows, :], output, ((1,), (0,))).astype(bf16).T
    cosine = cos_ref[...]
    sine = sin_ref[...]
    ones = jnp.ones((8, tokens), bf16)

    def rotate(block, direction):
        first, second = block[:HALF], block[HALF:ROT]
        return jnp.concatenate(
            [
                first * cosine - second * (direction * sine),
                second * cosine + first * (direction * sine),
                block[ROT:],
            ],
            axis=0,
        )

    def head(index, carry):
        start = pl.multiple_of(index * HD, HD)

        def rows(part):
            return pl.ds(part * width + start, HD)

        queries = rotate(qkv_ref[rows(0), :], 1.0).astype(bf16)
        keys = rotate(qkv_ref[rows(1), :], 1.0).astype(bf16)
        values = qkv_ref[rows(2), :].astype(bf16)
        queries = queries * jnp.asarray(scale, bf16)
        grads = grad_ref[pl.ds(start, HD), :]
        key_rows = keys.T
        value_rows = values.T
        dk_ref[...] = jnp.zeros(dk_ref.shape, f32)
        dv_ref[...] = jnp.zeros(dv_ref.shape, f32)
        for block in range(tokens // ROWS):
            begin, end = block * ROWS, (block + 1) * ROWS
            low = max(0, (begin - DOC_MAX + 1) // ROWS * ROWS)
            query = queries[:, begin:end]
            grad = grads[:, begin:end]
            scores = dot(key_rows[low:end], query, ((1,), (0,)))
            key_at = lax.broadcasted_iota(jnp.int32, scores.shape, 0) + low
            query_at = lax.broadcasted_iota(jnp.int32, scores.shape, 1) + begin
            allowed = (seg_col_ref[low:end, :] == seg_row_ref[:, begin:end]) & (
                key_at <= query_at
            )
            scores = jnp.where(allowed, scores, masked_score)
            highest = jnp.max(scores, axis=0, keepdims=True)
            exponent = jnp.exp(scores - highest)
            probs = exponent * (1.0 / jnp.sum(exponent, axis=0, keepdims=True))
            probs_b = probs.astype(bf16)
            attended = dot(values[:, low:end], probs_b, ((1,), (0,))).astype(bf16)
            feature_ref[rows(3), begin:end] = attended
            delta = jnp.sum(
                grad.astype(f32) * attended.astype(f32), axis=0, keepdims=True
            )
            grad_probs = dot(value_rows[low:end], grad, ((1,), (0,)))
            grad_scores = (probs * (grad_probs - delta)).astype(bf16)
            dq_ref[:, begin:end] = dot(keys[:, low:end], grad_scores, ((1,), (0,))) * scale
            dk_ref[:, low:end] += dot(query, grad_scores, ((1,), (1,)))
            dv_ref[:, low:end] += dot(grad, probs_b, ((1,), (1,)))
        for part, result in enumerate(
            (rotate(dq_ref[...], -1.0), rotate(dk_ref[...], -1.0), dv_ref[...])
        ):
            high = result.astype(bf16)
            feature_ref[rows(part), :] = high
            rest = (result - high.astype(f32)).astype(bf16)
            total = dot(ones, high, ((1,), (1,))) + dot(ones, rest, ((1,), (1,)))
            bias_grad_ref[pl.ds(part * (width // HD) + index, 1), :] = total[0:1]
        return carry

    bias_grad_ref[...] = jnp.zeros(bias_grad_ref.shape, f32)
    lax.fori_loop(0, width // HD, head, 0)

    begin = pl.multiple_of(ctx_ref[0] * (2 * width), 2 * width)
    part_one = dot(feature_ref[pl.ds(begin, width), :], first_ref[...], ((1,), (0,)))
    grad_weights_ref[:, :width] = part_one.astype(bf16).T

    @pl.when(ctx_ref[0] == 0)
    def _():
        keys_part = dot(feature_ref[width : 2 * width, :], first_ref[...], ((1,), (0,)))
        grad_weights_ref[:, width:] = keys_part.astype(bf16).T

    @pl.when(ctx_ref[0] != 0)
    def _():
        output_part = dot(feature_ref[3 * width :, :], cot_ref[...], ((1,), (0,)))
        grad_weights_ref[:, width:] = output_part.astype(bf16).T

    total_one = jnp.zeros((1, model), f32)
    total_two = jnp.zeros((1, model), f32)
    for rows in chunks:
        attended = feature_ref[3 * width :, rows].T
        mixed_ref[rows, :] = (0.5 * dot(attended, output, ((1,), (1,)))).astype(bf16)
        grad_first = 0.5 * dot(feature_ref[: 3 * width, rows].T, project, ((1,), (1,)))
        total_one += jnp.sum(grad_first * normed_ref[rows, :], axis=0, keepdims=True)
        total_two += jnp.sum(grad_first, axis=0, keepdims=True)
        grad_normed_ref[rows, :] = (grad_first * gain).astype(bf16)
    sums_ref[0:1, :] = total_one
    sums_ref[1:2, :] = total_two


def feed_kernel(
    ctx_ref, all_ref, normed_ref, cot_ref, vectors_ref, mixed_in_ref, grad_in_ref,
    mixed_ref, grad_normed_ref, grad_weights_ref, sums_ref, bias_grad_ref,
    up_ref, down_ref, second_ref, act_ref, pre_ref,
):
    tokens, model = normed_ref.shape
    shares, share, units = all_ref.shape[0], all_ref.shape[1] // 2, all_ref.shape[2]
    for s in range(shares):
        up_ref[s * share : (s + 1) * share, :] = all_ref[s, :share, :]
        down_ref[s * share : (s + 1) * share, :] = all_ref[s, share:, :]
    gain, shift = vectors_ref[2:3, :], vectors_ref[3:4, :]
    bias = jnp.where(
        ctx_ref[0] > 0, vectors_ref[6:7, units : 2 * units], vectors_ref[6:7, :units]
    )
    up, down = up_ref[...], down_ref[...]
    total_one = jnp.zeros((1, model), f32)
    total_two = jnp.zeros((1, model), f32)
    total_bias = jnp.zeros((1, units), f32)
    for i in range(0, tokens, ROWS):
        rows = slice(i, i + ROWS)
        second = (normed_ref[rows, :] * gain + shift).astype(bf16)
        second_ref[rows, :] = second
        preact = dot(second, up, ((1,), (0,))) + bias
        activated, slope = gelu_pair(preact)
        act = activated.astype(bf16)
        act_ref[:, rows] = act.T
        grad_pre = dot(cot_ref[rows, :], down, ((1,), (0,))) * slope
        total_bias += jnp.sum(grad_pre, axis=0, keepdims=True)
        pre = grad_pre.astype(bf16)
        pre_ref[:, rows] = pre.T
        mixed = dot(act, down, ((1,), (1,))) + mixed_in_ref[rows, :].astype(f32)
        mixed_ref[rows, :] = mixed.astype(bf16)
        grad_second = dot(pre, up, ((1,), (1,)))
        total_one += jnp.sum(grad_second * normed_ref[rows, :], axis=0, keepdims=True)
        total_two += jnp.sum(grad_second, axis=0, keepdims=True)
        grad_normed_ref[rows, :] = (
            grad_second * gain + grad_in_ref[rows, :].astype(f32)
        ).astype(bf16)
    sums_ref[0:1, :] = total_one
    sums_ref[1:2, :] = total_two
    bias_grad_ref[...] = total_bias
    up_part = dot(pre_ref[...], second_ref[...], ((1,), (0,))).astype(bf16).T
    down_part = dot(act_ref[...], cot_ref[...], ((1,), (0,))).astype(bf16).T
    for s in range(shares):
        grad_weights_ref[s, :share, :] = up_part[s * share : (s + 1) * share]
        grad_weights_ref[s, share:, :] = down_part[s * share : (s + 1) * share]


def call(kernel, out_shape, scratch, flops, name, *args):
    whole = pl.BlockSpec(memory_space=pltpu.VMEM)
    scalar = pl.BlockSpec(memory_space=pltpu.SMEM)
    moved = sum(a.size * a.dtype.itemsize for a in args)
    return pl.pallas_call(
        kernel,
        out_shape=[jax.ShapeDtypeStruct(shape, dtype) for shape, dtype in out_shape],
        in_specs=[scalar] + [whole] * (len(args) - 1),
        out_specs=[whole] * len(out_shape),
        scratch_shapes=[pltpu.VMEM(shape, dtype) for shape, dtype in scratch],
        cost_estimate=pl.CostEstimate(flops=flops, transcendentals=0, bytes_accessed=moved),
        name=name,
    )(*args)


def body(
    hidden_in, cotangent, segment_ids, attend_gain, attend_shift, feed_gain, feed_shift,
    project_weight, project_bias, output_weight, output_bias,
    upward_weight, upward_bias, downward_weight, downward_bias,
):
    n_dp, n_ctx, n_tensor = (lax.axis_size(a) for a in ("dp", "ctx", "tensor"))
    dp_index, ctx_index = lax.axis_index("dp"), lax.axis_index("ctx")
    second = ctx_index > 0
    share, _, width = project_weight.shape
    model = share * n_dp
    units = upward_weight.shape[1]
    half_units = units // n_ctx
    heads = width // HD

    def own_half(block, size, axis):
        return lax.dynamic_slice_in_dim(block, ctx_index * size, size, axis)

    hidden_all, hidden_first = gather_tokens(hidden_in[0])
    columns = 4 * width
    vectors = [
        attend_gain, attend_shift, feed_gain, feed_shift, output_bias, downward_bias,
        upward_bias[0],
    ]
    bias_share = HD // n_dp
    bias_wide = lax.dynamic_update_slice_in_dim(
        jnp.zeros((3, heads, HD), bf16), project_bias, dp_index * bias_share, 2
    )
    row = lax.broadcasted_iota(jnp.int32, (8, columns), 0)
    small = jnp.where(row == 7, jnp.pad(bias_wide.reshape(1, -1), ((0, 0), (0, width))), 0)
    for i, vector in enumerate(vectors):
        small = jnp.where(row == i, jnp.pad(vector, (0, columns - share))[None, :], small)
    attention_all = gather_dp(
        jnp.concatenate(
            [
                jnp.concatenate(
                    [project_weight.reshape(share, 3 * width), output_weight.T], axis=1
                ),
                small,
            ],
            axis=0,
        )
    )
    feed_all = gather_dp(
        jnp.concatenate(
            [own_half(upward_weight, half_units, 1), own_half(downward_weight, half_units, 0).T],
            axis=0,
        )
    )
    if share % 32:
        tail = attention_all[:, share:]
        tail = jnp.concatenate(
            [
                tail[:, :7, :share].transpose(1, 0, 2).reshape(7, model),
                jnp.sum(tail[:, 7], axis=0, keepdims=True),
            ],
            axis=0,
        )
        attention_all = jnp.concatenate(
            [attention_all[:, :share].reshape(model, columns), tail], axis=0
        )[None]
        feed_all = feed_all.reshape(n_dp, 2, share, half_units).transpose(1, 0, 2, 3)
        feed_all = feed_all.reshape(1, 2 * model, half_units)

    hidden_rows = hidden_in[0]
    grad_rows = cotangent[0]
    grad_source, _ = lax.optimization_barrier((grad_rows, hidden_first))
    grad_all, _ = gather_tokens(grad_source)
    tokens = hidden_all.shape[0]

    source = hidden_all.astype(f32)
    centred = source - jnp.mean(source, axis=-1, keepdims=True)
    inverse = lax.rsqrt(jnp.mean(centred * centred, axis=-1, keepdims=True) + epsilon)
    normed = centred * inverse

    frequency = 10000.0 ** (-2.0 * jnp.arange(HALF, dtype=f32) / ROT)
    angles = frequency[:, None] * jnp.arange(tokens, dtype=f32)[None, :]
    ctx_scalar = ctx_index.reshape(1).astype(jnp.int32)
    segments = segment_ids[0]
    vectors, mixed, grad_normed, grad_attention, attention_sums, project_bias_grad = call(
        attention_kernel,
        [
            ((8, model), f32), ((tokens, model), bf16), ((tokens, model), bf16),
            ((model, 2 * width), bf16), ((2, model), f32), ((16, HD), f32),
        ],
        [
            ((model, columns), bf16), ((tokens, model), bf16), ((3 * width, tokens), f32),
            ((width, tokens), bf16), ((columns, tokens), bf16),
            ((HD, tokens), f32), ((HD, tokens), f32), ((HD, tokens), f32),
        ],
        tokens * model * columns * 8,
        "attention_part",
        ctx_scalar, attention_all, normed, grad_all, jnp.cos(angles), jnp.sin(angles),
        segments[None, :], segments[:, None],
    )
    attention_parts = exchange_dp(grad_attention.reshape(n_dp, share, 2 * width))

    mixed, grad_normed, grad_feed, feed_sums, upward_bias_grad = call(
        feed_kernel,
        [
            ((tokens, model), bf16), ((tokens, model), bf16), (feed_all.shape, bf16),
            ((2, model), f32), ((1, half_units), f32),
        ],
        [
            ((model, half_units), bf16), ((model, half_units), bf16), ((tokens, model), bf16),
            ((half_units, tokens), bf16), ((half_units, tokens), bf16),
        ],
        tokens * model * half_units * 12,
        "feed_part",
        ctx_scalar, feed_all, normed, grad_all, vectors, mixed, grad_normed,
    )
    if share % 32:
        grad_feed = grad_feed.reshape(2, n_dp, share, half_units).transpose(1, 0, 2, 3)
        grad_feed = grad_feed.reshape(n_dp, 2 * share, half_units)
    grad_feed, attention_parts = lax.optimization_barrier((grad_feed, attention_parts))
    feed_parts = exchange_dp(grad_feed)

    mixed = halve_rows(mixed)
    grad_normed = halve_rows(grad_normed)

    tensor_index = lax.axis_index("tensor")
    project_row = 0.5 * project_bias_grad[: 3 * heads].reshape(1, 3 * width)
    project_row = jnp.pad(project_row, ((0, 0), (0, model - 3 * width)))
    unit_row = jnp.where(
        second,
        jnp.pad(upward_bias_grad, ((0, 0), (half_units, 0))),
        jnp.pad(upward_bias_grad, ((0, 0), (0, half_units))),
    )
    slot = lax.broadcasted_iota(jnp.int32, (n_tensor, 1), 0) == tensor_index
    sums = jnp.concatenate(
        [
            attention_sums,
            feed_sums,
            jnp.sum(grad_rows.astype(f32), axis=0, keepdims=True),
            jnp.where(slot, project_row, 0.0),
            jnp.where(slot, unit_row, 0.0),
        ],
        axis=0,
    )
    sums = total_over(sums, ("tensor", "ctx", "dp"))
    shared = lax.dynamic_slice_in_dim(sums[:5], dp_index * share, share, 1)
    project_sum = lax.dynamic_index_in_dim(sums, 5 + tensor_index, 0, keepdims=False)
    project_bias_grad = lax.dynamic_slice_in_dim(
        project_sum[: 3 * width].reshape(3, heads, HD), dp_index * bias_share, bias_share, 2
    )
    upward_bias_grad = lax.dynamic_slice(
        sums, (5 + n_tensor + tensor_index, dp_index * (units // n_dp)), (1, units // n_dp)
    )

    own_source = hidden_rows.astype(f32)
    hidden_out = own_source + mixed
    hidden_out = (hidden_out + (vectors[4] + vectors[5])).astype(bf16)[None]

    own_centred = own_source - jnp.mean(own_source, axis=-1, keepdims=True)
    own_inverse = lax.rsqrt(jnp.mean(own_centred * own_centred, axis=-1, keepdims=True) + epsilon)
    own_normed = own_centred * own_inverse
    grad_inner = own_inverse * (
        grad_normed
        - jnp.mean(grad_normed, axis=-1, keepdims=True)
        - own_normed * jnp.mean(grad_normed * own_normed, axis=-1, keepdims=True)
    )
    hidden_grad = (grad_rows.astype(f32) + grad_inner).astype(bf16)[None]

    attention_sum = jnp.sum(attention_parts.astype(f32), axis=0)
    attention_own = lax.reduce_precision(attention_sum, 8, 7).astype(bf16)
    attention_both = joined(attention_own, flipped(attention_own, "ctx", 1), second).astype(f32)

    feed_sum = jnp.sum(feed_parts.astype(f32), axis=0)
    feed_own = lax.reduce_precision(feed_sum, 8, 7).astype(bf16)
    feed_both = joined(feed_own, flipped(feed_own, "ctx", 1), second).astype(f32)

    return (
        hidden_out,
        hidden_grad,
        shared[0],
        shared[1],
        shared[2],
        shared[3],
        attention_both[:, : 3 * width].reshape(share, 3, width),
        project_bias_grad,
        attention_both[:, 3 * width :].T,
        shared[4],
        feed_both[:share],
        upward_bias_grad,
        feed_both[share:].T,
        shared[4],
    )


def solution(mesh):
    rows = P("dp", ("ctx", "tensor"), None)
    in_specs = (
        rows, rows, P("dp", None), P("dp"), P("dp"), P("dp"), P("dp"),
        P("dp", None, "tensor"), P(None, "tensor", "dp"), P("tensor", "dp"), P("dp"),
        P("dp", "tensor"), P("tensor", "dp"), P("tensor", "dp"), P("dp"),
    )
    out_specs = (
        rows, rows, P("dp"), P("dp"), P("dp"), P("dp"),
        P("dp", None, "tensor"), P(None, "tensor", "dp"), P("tensor", "dp"), P("dp"),
        P("dp", "tensor"), P("tensor", "dp"), P("tensor", "dp"), P("dp"),
    )
    return jax.shard_map(body, mesh=mesh, in_specs=in_specs, out_specs=out_specs, check_vma=False)
```

```python
import functools

import jax
import jax.numpy as jnp
from jax import lax
from jax.experimental import pallas as pl
from jax.experimental.pallas import tpu as pltpu
from jax.sharding import PartitionSpec as P

HD = 64
ROT = 16
HALF = ROT // 2
DOC_MAX = 512
ROWS = 256

epsilon = 1e-05
masked_score = -1e30
f32 = jnp.float32
bf16 = jnp.bfloat16


def flipped(block, axis, bit):
    return lax.ppermute(block, axis, [(i, i ^ bit) for i in range(lax.axis_size(axis))])


def ordered(own, other, second, dim):
    return jnp.where(
        second, jnp.stack([other, own], axis=dim), jnp.stack([own, other], axis=dim)
    )


def joined(own, other, second):
    return jnp.where(
        second, jnp.concatenate([other, own], axis=1), jnp.concatenate([own, other], axis=1)
    )


def gather_tokens(rows, ctx_first):
    steps = [("ctx", 1, 0), ("tensor", 2, 1)] if ctx_first else [("tensor", 2, 0), ("ctx", 1, 0)]
    block = rows
    for axis, bit, dim in steps + [("tensor", 1, 2)]:
        upper = (lax.axis_index(axis) & bit) > 0
        block = ordered(block, flipped(block, axis, bit), upper, dim)
    return block.reshape(-1, rows.shape[-1])


def shifted(block, distance):
    count = lax.axis_size("dp")
    return lax.ppermute(block, "dp", [(i, (i + distance) % count) for i in range(count)])


def exchange_dp(blocks):
    return lax.all_to_all(blocks, "dp", 0, 0)


def gelu_pair(preact):
    cumulative = 0.5 * (1.0 + jax.scipy.special.erf(preact * 0.7071067811865476))
    density = jnp.exp(-0.5 * preact * preact) * 0.3989422804014327
    return (preact * cumulative, cumulative + preact * density)


def dot(left, right, dims):
    return lax.dot_general(left, right, (dims, ((), ())), preferred_element_type=f32)


def pack_kernel(dp_ref, project_ref, output_ref, bias_ref, *refs):
    vector_refs, packed_ref = refs[:-1], refs[-1]
    _, share, width = project_ref.shape
    _, heads, part = bias_ref.shape
    for i in range(3):
        packed_ref[:share, i * width : (i + 1) * width] = project_ref[i]
    packed_ref[:share, 3 * width :] = output_ref[...].T
    rest = jnp.zeros((1, 4 * width - share), f32)
    rows = [
        jnp.concatenate([ref[...].astype(f32).reshape(1, share), rest], axis=1)
        for ref in vector_refs
    ]
    lane = lax.broadcasted_iota(jnp.int32, (1, HD), 1)
    own = (lane >= dp_ref[0] * part) & (lane < (dp_ref[0] + 1) * part)
    pieces = []
    for kind in range(3):
        for head in range(heads):
            piece = bias_ref[kind, head : head + 1, :].astype(f32)
            pieces.append(jnp.where(own, jnp.concatenate([piece] * (HD // part), axis=1), 0.0))
    rows.append(jnp.concatenate(pieces + [jnp.zeros((1, width), f32)], axis=1))
    packed_ref[share:, :] = jnp.concatenate(rows, axis=0).astype(bf16)


def pack_feed_kernel(ctx_ref, up_ref, down_ref, packed_ref):
    share, units = up_ref.shape
    for half in range(2):

        @pl.when(ctx_ref[0] == half)
        def _():
            lanes = slice(half * (units // 2), (half + 1) * (units // 2))
            for copy in range(packed_ref.shape[0]):
                packed_ref[copy, :share, :] = up_ref[:, lanes]
                packed_ref[copy, share:, :] = down_ref[:, lanes]


def rows_at(index, size):
    return pl.ds(pl.multiple_of(index * size, size), size)


def split_kernel(
    bits_ref, kept_ref, got_ref, mixed_kept_ref, mixed_away_ref, grad_kept_ref, grad_away_ref
):
    size = kept_ref.shape[1] // 4
    high, ctx = bits_ref[0], bits_ref[1]

    def total(which, c, h):
        rows = rows_at(c * 2 + h, size)
        both = kept_ref[which, rows, :].astype(f32) + got_ref[which, rows, :].astype(f32)
        return both.astype(bf16)

    for i in range(2):
        rows = slice(i * size, (i + 1) * size)
        mixed_kept_ref[rows, :] = total(0, i, high)
        mixed_away_ref[rows, :] = total(0, i, 1 - high)
        grad_kept_ref[rows, :] = total(1, ctx, i)
        grad_away_ref[rows, :] = total(1, 1 - ctx, i)


def halve_kernel(bit_ref, kept_ref, got_ref, kept_out_ref, away_out_ref):
    size = kept_ref.shape[0] // 2

    def total(half):
        rows = rows_at(half, size)
        return kept_ref[rows, :].astype(f32) + got_ref[rows, :].astype(f32)

    kept_out_ref[...] = total(bit_ref[0])
    away_out_ref[...] = total(1 - bit_ref[0]).astype(bf16)


def attention_kernel(shares, place_ref, *refs):
    piece_refs, refs = refs[:shares], refs[shares:]
    normed_ref, cot_ref, cos_ref, sin_ref, seg_row_ref, seg_col_ref = refs[:6]
    refs = refs[6:]
    vectors_ref, mixed_ref, grad_normed_ref, sums_ref, bias_grad_ref = refs[:5]
    part_refs, refs = refs[5 : 5 + shares], refs[5 + shares :]
    (
        weights_ref, small_ref, first_ref, qkv_ref, grad_ref, feature_ref, grad_weights_ref,
        dq_ref, dk_ref, dv_ref,
    ) = refs
    tokens, model = normed_ref.shape
    share = piece_refs[0].shape[0] - 8
    width = grad_ref.shape[0]
    scale = HD**-0.5
    ctx, dp = place_ref[0], place_ref[1]
    for d, ref in enumerate(piece_refs):
        source = lax.rem(dp + (shares - d), shares)
        weights_ref[rows_at(source, share), :] = ref[:share, :]
        small_ref[source] = ref[share:, :].astype(f32)
    small = [small_ref[i] for i in range(shares)]
    vectors = jnp.concatenate([piece[:, :share] for piece in small], axis=1)
    vectors_ref[...] = vectors
    bias = sum(piece[7:8, : 3 * width] for piece in small)
    gain, shift = vectors[0:1], vectors[1:2]
    project = weights_ref[:, : 3 * width]
    output = weights_ref[:, 3 * width :]
    chunks = [slice(i, i + ROWS) for i in range(0, tokens, ROWS)]
    for rows in chunks:
        first = (normed_ref[rows, :] * gain + shift).astype(bf16)
        first_ref[rows, :] = first
        qkv_ref[:, rows] = (dot(first, project, ((1,), (0,))) + bias).T
        grad_ref[:, rows] = dot(cot_ref[rows, :], output, ((1,), (0,))).astype(bf16).T
    cosine = cos_ref[...]
    sine = sin_ref[...]
    ones = jnp.ones((8, tokens), bf16)

    def rotate(block, direction):
        first, second = block[:HALF], block[HALF:ROT]
        return jnp.concatenate(
            [
                first * cosine - second * (direction * sine),
                second * cosine + first * (direction * sine),
                block[ROT:],
            ],
            axis=0,
        )

    def head(index, carry):
        start = pl.multiple_of(index * HD, HD)

        def rows(part):
            return pl.ds(part * width + start, HD)

        queries = rotate(qkv_ref[rows(0), :], 1.0).astype(bf16)
        keys = rotate(qkv_ref[rows(1), :], 1.0).astype(bf16)
        values = qkv_ref[rows(2), :].astype(bf16)
        queries = queries * jnp.asarray(scale, bf16)
        grads = grad_ref[pl.ds(start, HD), :]
        key_rows = keys.T
        value_rows = values.T
        dk_ref[...] = jnp.zeros(dk_ref.shape, f32)
        dv_ref[...] = jnp.zeros(dv_ref.shape, f32)
        for block in range(tokens // ROWS):
            begin, end = block * ROWS, (block + 1) * ROWS
            low = max(0, (begin - DOC_MAX + 1) // ROWS * ROWS)
            query = queries[:, begin:end]
            grad = grads[:, begin:end]
            scores = dot(key_rows[low:end], query, ((1,), (0,)))
            key_at = lax.broadcasted_iota(jnp.int32, scores.shape, 0) + low
            query_at = lax.broadcasted_iota(jnp.int32, scores.shape, 1) + begin
            allowed = (seg_col_ref[low:end, :] == seg_row_ref[:, begin:end]) & (
                key_at <= query_at
            )
            scores = jnp.where(allowed, scores, masked_score)
            highest = jnp.max(scores, axis=0, keepdims=True)
            exponent = jnp.exp(scores - highest)
            probs = exponent * (1.0 / jnp.sum(exponent, axis=0, keepdims=True))
            probs_b = probs.astype(bf16)
            attended = dot(values[:, low:end], probs_b, ((1,), (0,))).astype(bf16)
            feature_ref[rows(3), begin:end] = attended
            delta = jnp.sum(
                grad.astype(f32) * attended.astype(f32), axis=0, keepdims=True
            )
            grad_probs = dot(value_rows[low:end], grad, ((1,), (0,)))
            grad_scores = (probs * (grad_probs - delta)).astype(bf16)
            dq_ref[:, begin:end] = dot(keys[:, low:end], grad_scores, ((1,), (0,))) * scale
            dk_ref[:, low:end] += dot(query, grad_scores, ((1,), (1,)))
            dv_ref[:, low:end] += dot(grad, probs_b, ((1,), (1,)))
        for part, result in enumerate(
            (rotate(dq_ref[...], -1.0), rotate(dk_ref[...], -1.0), dv_ref[...])
        ):
            high = result.astype(bf16)
            feature_ref[rows(part), :] = high
            rest = (result - high.astype(f32)).astype(bf16)
            total = dot(ones, high, ((1,), (1,))) + dot(ones, rest, ((1,), (1,)))
            bias_grad_ref[pl.ds(part * (width // HD) + index, 1), :] = total[0:1]
        return carry

    bias_grad_ref[...] = jnp.zeros(bias_grad_ref.shape, f32)
    lax.fori_loop(0, width // HD, head, 0)

    begin = pl.multiple_of(ctx * (2 * width), 2 * width)
    part_one = dot(feature_ref[pl.ds(begin, width), :], first_ref[...], ((1,), (0,)))
    grad_weights_ref[:, :width] = part_one.astype(bf16).T

    @pl.when(ctx == 0)
    def _():
        keys_part = dot(feature_ref[width : 2 * width, :], first_ref[...], ((1,), (0,)))
        grad_weights_ref[:, width:] = keys_part.astype(bf16).T

    @pl.when(ctx != 0)
    def _():
        output_part = dot(feature_ref[3 * width :, :], cot_ref[...], ((1,), (0,)))
        grad_weights_ref[:, width:] = output_part.astype(bf16).T

    for d, ref in enumerate(part_refs):
        ref[...] = grad_weights_ref[rows_at(lax.rem(dp + d, shares), share), :]

    total_one = jnp.zeros((1, model), f32)
    total_two = jnp.zeros((1, model), f32)
    for rows in chunks:
        attended = feature_ref[3 * width :, rows].T
        mixed_ref[rows, :] = (0.5 * dot(attended, output, ((1,), (1,)))).astype(bf16)
        grad_first = 0.5 * dot(feature_ref[: 3 * width, rows].T, project, ((1,), (1,)))
        total_one += jnp.sum(grad_first * normed_ref[rows, :], axis=0, keepdims=True)
        total_two += jnp.sum(grad_first, axis=0, keepdims=True)
        grad_normed_ref[rows, :] = (grad_first * gain).astype(bf16)
    sums_ref[0:1, :] = total_one
    sums_ref[1:2, :] = total_two


def feed_kernel(
    ctx_ref, all_ref, normed_ref, cot_ref, vectors_ref, mixed_in_ref, grad_in_ref,
    kept_ref, away_ref, grad_weights_ref, sums_ref, bias_grad_ref,
    up_ref, down_ref, second_ref, act_ref, pre_ref,
):
    tokens, model = normed_ref.shape
    shares, share, units = all_ref.shape[0], all_ref.shape[1] // 2, all_ref.shape[2]
    for s in range(shares):
        up_ref[s * share : (s + 1) * share, :] = all_ref[s, :share, :]
        down_ref[s * share : (s + 1) * share, :] = all_ref[s, share:, :]
    gain, shift = vectors_ref[2:3, :], vectors_ref[3:4, :]
    bias = jnp.where(
        ctx_ref[0] > 0, vectors_ref[6:7, units : 2 * units], vectors_ref[6:7, :units]
    )
    up, down = up_ref[...], down_ref[...]
    low = ctx_ref[1] > 0

    def divide(which, start, block):
        first, last = block[: ROWS // 2], block[ROWS // 2 :]
        rows = slice(start // 2, start // 2 + ROWS // 2)
        kept_ref[which, rows, :] = jnp.where(low, last, first)
        away_ref[which, rows, :] = jnp.where(low, first, last)

    total_one = jnp.zeros((1, model), f32)
    total_two = jnp.zeros((1, model), f32)
    total_bias = jnp.zeros((1, units), f32)
    for i in range(0, tokens, ROWS):
        rows = slice(i, i + ROWS)
        second = (normed_ref[rows, :] * gain + shift).astype(bf16)
        second_ref[rows, :] = second
        preact = dot(second, up, ((1,), (0,))) + bias
        activated, slope = gelu_pair(preact)
        act = activated.astype(bf16)
        act_ref[:, rows] = act.T
        grad_pre = dot(cot_ref[rows, :], down, ((1,), (0,))) * slope
        total_bias += jnp.sum(grad_pre, axis=0, keepdims=True)
        pre = grad_pre.astype(bf16)
        pre_ref[:, rows] = pre.T
        mixed = dot(act, down, ((1,), (1,))) + mixed_in_ref[rows, :].astype(f32)
        divide(0, i, mixed.astype(bf16))
        grad_second = dot(pre, up, ((1,), (1,)))
        total_one += jnp.sum(grad_second * normed_ref[rows, :], axis=0, keepdims=True)
        total_two += jnp.sum(grad_second, axis=0, keepdims=True)
        grad_normed = grad_second * gain + grad_in_ref[rows, :].astype(f32)
        divide(1, i, grad_normed.astype(bf16))
    sums_ref[0:1, :] = total_one
    sums_ref[1:2, :] = total_two
    bias_grad_ref[...] = total_bias
    up_part = dot(pre_ref[...], second_ref[...], ((1,), (0,))).astype(bf16).T
    down_part = dot(act_ref[...], cot_ref[...], ((1,), (0,))).astype(bf16).T
    for s in range(shares):
        grad_weights_ref[s, :share, :] = up_part[s * share : (s + 1) * share]
        grad_weights_ref[s, share:, :] = down_part[s * share : (s + 1) * share]


def call(kernel, out_shape, scratch, flops, name, *args):
    whole = pl.BlockSpec(memory_space=pltpu.VMEM)
    scalar = pl.BlockSpec(memory_space=pltpu.SMEM)
    moved = sum(a.size * a.dtype.itemsize for a in args)
    return pl.pallas_call(
        kernel,
        out_shape=[jax.ShapeDtypeStruct(shape, dtype) for shape, dtype in out_shape],
        in_specs=[scalar] + [whole] * (len(args) - 1),
        out_specs=[whole] * len(out_shape),
        scratch_shapes=[pltpu.VMEM(shape, dtype) for shape, dtype in scratch],
        cost_estimate=pl.CostEstimate(flops=flops, transcendentals=0, bytes_accessed=moved),
        name=name,
    )(*args)


def body(
    hidden_in, cotangent, segment_ids, attend_gain, attend_shift, feed_gain, feed_shift,
    project_weight, project_bias, output_weight, output_bias,
    upward_weight, upward_bias, downward_weight, downward_bias,
):
    n_dp, n_ctx, n_tensor = (lax.axis_size(a) for a in ("dp", "ctx", "tensor"))
    dp_index, ctx_index = lax.axis_index("dp"), lax.axis_index("ctx")
    second = ctx_index > 0
    share, _, width = project_weight.shape
    model = share * n_dp
    units = upward_weight.shape[1]
    half_units = units // n_ctx
    heads = width // HD

    hidden_all = gather_tokens(hidden_in[0], True)
    columns = 4 * width
    bias_share = HD // n_dp
    tensor_index = lax.axis_index("tensor")

    def scalars(*values):
        return jnp.stack([jnp.asarray(v, jnp.int32) for v in values])

    (packed,) = call(
        pack_kernel, [((share + 8, columns), bf16)], [], 0, "pack_attention",
        scalars(dp_index), project_weight.transpose(1, 0, 2), output_weight, project_bias,
        attend_gain, attend_shift, feed_gain, feed_shift, output_bias, downward_bias,
        upward_bias[0],
    )
    (feed_block,) = call(
        pack_feed_kernel, [((n_dp, 2 * share, half_units), bf16)], [], 0, "pack_feed",
        scalars(ctx_index), upward_weight, downward_weight.T,
    )
    few = n_dp <= 4
    if few:
        pieces = [packed] + [shifted(packed, d) for d in range(1, n_dp)]
    else:
        everything = exchange_dp(jnp.broadcast_to(packed[None], (n_dp,) + packed.shape))
        tail = everything[:, share:]
        tail = jnp.concatenate(
            [
                tail[:, :7, :share].transpose(1, 0, 2).reshape(7, model),
                jnp.sum(tail[:, 7], axis=0, keepdims=True),
            ],
            axis=0,
        )
        pieces = [
            jnp.concatenate([everything[:, :share].reshape(model, columns), tail], axis=0)
        ]
    shares = len(pieces)
    feed_block, hidden_all = lax.optimization_barrier((feed_block, hidden_all))
    feed_all = exchange_dp(feed_block)
    if not few:
        feed_all = feed_all.reshape(n_dp, 2, share, half_units).transpose(1, 0, 2, 3)
        feed_all = feed_all.reshape(1, 2 * model, half_units)

    hidden_rows = hidden_in[0]
    grad_rows = cotangent[0]
    grad_all = gather_tokens(grad_rows, False)
    tokens = hidden_all.shape[0]

    source = hidden_all.astype(f32)
    centred = source - jnp.mean(source, axis=-1, keepdims=True)
    inverse = lax.rsqrt(jnp.mean(centred * centred, axis=-1, keepdims=True) + epsilon)
    normed = centred * inverse

    frequency = 10000.0 ** (-2.0 * jnp.arange(HALF, dtype=f32) / ROT)
    angles = frequency[:, None] * jnp.arange(tokens, dtype=f32)[None, :]
    segments = segment_ids[0]
    vectors, mixed, grad_normed, attention_sums, project_bias_grad, *attention_parts = call(
        functools.partial(attention_kernel, shares),
        [
            ((8, model), f32), ((tokens, model), bf16), ((tokens, model), bf16),
            ((2, model), f32), ((16, HD), f32),
        ]
        + [((model // shares, 2 * width), bf16)] * shares,
        [
            ((model, columns), bf16), ((shares, 8, columns), f32), ((tokens, model), bf16),
            ((3 * width, tokens), f32), ((width, tokens), bf16), ((columns, tokens), bf16),
            ((model, 2 * width), bf16),
            ((HD, tokens), f32), ((HD, tokens), f32), ((HD, tokens), f32),
        ],
        tokens * model * columns * 8,
        "attention_part",
        scalars(ctx_index, dp_index if few else 0), *pieces, normed, grad_all,
        jnp.cos(angles), jnp.sin(angles), segments[None, :], segments[:, None],
    )
    if few:
        attention_parts = attention_parts[:1] + [
            shifted(attention_parts[d], d) for d in range(1, n_dp)
        ]
    else:
        exchanged = exchange_dp(attention_parts[0].reshape(n_dp, share, 2 * width))
        attention_parts = [exchanged[i] for i in range(n_dp)]

    kept, away, grad_feed, feed_sums, upward_bias_grad = call(
        feed_kernel,
        [
            ((2, tokens // 2, model), bf16), ((2, tokens // 2, model), bf16),
            (feed_all.shape, bf16), ((2, model), f32), ((1, half_units), f32),
        ],
        [
            ((model, half_units), bf16), ((model, half_units), bf16), ((tokens, model), bf16),
            ((half_units, tokens), bf16), ((half_units, tokens), bf16),
        ],
        tokens * model * half_units * 12,
        "feed_part",
        scalars(ctx_index, tensor_index % 2),
        feed_all, normed, grad_all, vectors, mixed, grad_normed,
    )
    kept, away, grad_feed, feed_sums, upward_bias_grad, attention_parts = (
        lax.optimization_barrier(
            (kept, away, grad_feed, feed_sums, upward_bias_grad, attention_parts)
        )
    )
    if not few:
        grad_feed = grad_feed.reshape(2, n_dp, share, half_units).transpose(1, 0, 2, 3)
        grad_feed = grad_feed.reshape(n_dp, 2 * share, half_units)
    feed_parts = exchange_dp(grad_feed)

    project_row = 0.5 * project_bias_grad[: 3 * heads].reshape(1, 3 * width)
    project_row = jnp.pad(project_row, ((0, 0), (0, model - 3 * width)))
    unit_row = jnp.where(
        second,
        jnp.pad(upward_bias_grad, ((0, 0), (half_units, 0))),
        jnp.pad(upward_bias_grad, ((0, 0), (0, half_units))),
    )
    slot = lax.broadcasted_iota(jnp.int32, (n_tensor, 1), 0) == tensor_index
    sums = jnp.concatenate(
        [
            attention_sums,
            feed_sums,
            jnp.sum(grad_rows.astype(f32), axis=0, keepdims=True),
            jnp.where(slot, project_row, 0.0),
            jnp.where(slot, unit_row, 0.0),
        ],
        axis=0,
    )
    def added(values, axis, bit):
        return values + flipped(values, axis, bit)

    high_bit = tensor_index // 2
    quarter = ((tokens // 4, model), bf16)
    away, sums = lax.optimization_barrier(
        (flipped(away, "tensor", 1), added(sums, "tensor", 1))
    )
    mixed_kept, mixed_away, grad_kept, grad_away = call(
        split_kernel, [quarter] * 4, [], 0, "split",
        scalars(high_bit, ctx_index), kept, away,
    )
    sums = added(added(sums, "tensor", 2), "ctx", 1)
    grad_away, sums = lax.optimization_barrier((flipped(grad_away, "ctx", 1), sums))
    eighths = [((tokens // 8, model), f32), ((tokens // 8, model), bf16)]
    grad_normed, grad_away = call(
        halve_kernel, eighths, [], 0, "halve_grad", scalars(high_bit), grad_kept, grad_away
    )
    mixed, mixed_away = call(
        halve_kernel, eighths, [], 0, "halve_mixed",
        scalars(ctx_index), mixed_kept, flipped(mixed_away, "tensor", 2),
    )
    bit = 1
    while bit < n_dp:
        sums = added(sums, "dp", bit)
        bit *= 2
    mixed = mixed + flipped(mixed_away, "ctx", 1).astype(f32)
    grad_normed = grad_normed + flipped(grad_away, "tensor", 2).astype(f32)
    mixed, grad_normed, sums, feed_parts = lax.optimization_barrier(
        (mixed, grad_normed, sums, feed_parts)
    )
    shared = lax.dynamic_slice_in_dim(sums[:5], dp_index * share, share, 1)
    project_sum = lax.dynamic_index_in_dim(sums, 5 + tensor_index, 0, keepdims=False)
    project_bias_grad = lax.dynamic_slice_in_dim(
        project_sum[: 3 * width].reshape(3, heads, HD), dp_index * bias_share, bias_share, 2
    )
    upward_bias_grad = lax.dynamic_slice(
        sums, (5 + n_tensor + tensor_index, dp_index * (units // n_dp)), (1, units // n_dp)
    )

    own_source = hidden_rows.astype(f32)
    hidden_out = own_source + mixed
    hidden_out = (hidden_out + (vectors[4] + vectors[5])).astype(bf16)[None]

    own_centred = own_source - jnp.mean(own_source, axis=-1, keepdims=True)
    own_inverse = lax.rsqrt(jnp.mean(own_centred * own_centred, axis=-1, keepdims=True) + epsilon)
    own_normed = own_centred * own_inverse
    grad_inner = own_inverse * (
        grad_normed
        - jnp.mean(grad_normed, axis=-1, keepdims=True)
        - own_normed * jnp.mean(grad_normed * own_normed, axis=-1, keepdims=True)
    )
    hidden_grad = (grad_rows.astype(f32) + grad_inner).astype(bf16)[None]

    attention_sum = sum(part.astype(f32) for part in attention_parts)
    attention_own = lax.reduce_precision(attention_sum, 8, 7).astype(bf16)
    attention_both = joined(attention_own, flipped(attention_own, "ctx", 1), second).astype(f32)

    feed_sum = jnp.sum(feed_parts.astype(f32), axis=0)
    feed_own = lax.reduce_precision(feed_sum, 8, 7).astype(bf16)
    feed_both = joined(feed_own, flipped(feed_own, "ctx", 1), second).astype(f32)

    return (
        hidden_out,
        hidden_grad,
        shared[0],
        shared[1],
        shared[2],
        shared[3],
        attention_both[:, : 3 * width].reshape(share, 3, width),
        project_bias_grad,
        attention_both[:, 3 * width :].T,
        shared[4],
        feed_both[:share],
        upward_bias_grad,
        feed_both[share:].T,
        shared[4],
    )


def solution(mesh):
    rows = P("dp", ("ctx", "tensor"), None)
    in_specs = (
        rows, rows, P("dp", None), P("dp"), P("dp"), P("dp"), P("dp"),
        P("dp", None, "tensor"), P(None, "tensor", "dp"), P("tensor", "dp"), P("dp"),
        P("dp", "tensor"), P("tensor", "dp"), P("tensor", "dp"), P("dp"),
    )
    out_specs = (
        rows, rows, P("dp"), P("dp"), P("dp"), P("dp"),
        P("dp", None, "tensor"), P(None, "tensor", "dp"), P("tensor", "dp"), P("dp"),
        P("dp", "tensor"), P("tensor", "dp"), P("tensor", "dp"), P("dp"),
    )
    return jax.shard_map(body, mesh=mesh, in_specs=in_specs, out_specs=out_specs, check_vma=False)
```

```python
import functools

import jax
import jax.numpy as jnp
from jax import lax
from jax.experimental import pallas as pl
from jax.experimental.pallas import tpu as pltpu
from jax.sharding import PartitionSpec as P

HD = 64
ROT = 16
HALF = ROT // 2
DOC_MAX = 512
ROWS = 256

epsilon = 1e-05
masked_score = -1e30
f32 = jnp.float32
bf16 = jnp.bfloat16


def flipped(block, axis, bit):
    return lax.ppermute(block, axis, [(i, i ^ bit) for i in range(lax.axis_size(axis))])


def ordered(own, other, second, dim):
    return jnp.where(
        second, jnp.stack([other, own], axis=dim), jnp.stack([own, other], axis=dim)
    )


def joined(own, other, second):
    return jnp.where(
        second, jnp.concatenate([other, own], axis=1), jnp.concatenate([own, other], axis=1)
    )


def gather_tokens(rows, ctx_first):
    steps = [("ctx", 1, 0), ("tensor", 2, 1)] if ctx_first else [("tensor", 2, 0), ("ctx", 1, 0)]
    block = rows
    for axis, bit, dim in steps + [("tensor", 1, 2)]:
        upper = (lax.axis_index(axis) & bit) > 0
        block = ordered(block, flipped(block, axis, bit), upper, dim)
    return block.reshape(-1, rows.shape[-1])


def shifted(block, distance):
    count = lax.axis_size("dp")
    return lax.ppermute(block, "dp", [(i, (i + distance) % count) for i in range(count)])


def exchange_dp(blocks):
    return lax.all_to_all(blocks, "dp", 0, 0)


def gelu_pair(preact):
    cumulative = 0.5 * (1.0 + jax.scipy.special.erf(preact * 0.7071067811865476))
    density = jnp.exp(-0.5 * preact * preact) * 0.3989422804014327
    return (preact * cumulative, cumulative + preact * density)


def dot(left, right, dims):
    return lax.dot_general(left, right, (dims, ((), ())), preferred_element_type=f32)


def pack_kernel(dp_ref, project_ref, output_ref, bias_ref, *refs):
    vector_refs, packed_ref = refs[:-1], refs[-1]
    _, share, width = project_ref.shape
    _, heads, part = bias_ref.shape
    for i in range(3):
        packed_ref[:share, i * width : (i + 1) * width] = project_ref[i]
    packed_ref[:share, 3 * width :] = output_ref[...].T
    rest = jnp.zeros((1, 4 * width - share), f32)
    rows = [
        jnp.concatenate([ref[...].astype(f32).reshape(1, share), rest], axis=1)
        for ref in vector_refs
    ]
    lane = lax.broadcasted_iota(jnp.int32, (1, HD), 1)
    own = (lane >= dp_ref[0] * part) & (lane < (dp_ref[0] + 1) * part)
    pieces = []
    for kind in range(3):
        for head in range(heads):
            piece = bias_ref[kind, head : head + 1, :].astype(f32)
            pieces.append(jnp.where(own, jnp.concatenate([piece] * (HD // part), axis=1), 0.0))
    rows.append(jnp.concatenate(pieces + [jnp.zeros((1, width), f32)], axis=1))
    packed_ref[share:, :] = jnp.concatenate(rows, axis=0).astype(bf16)


def pack_feed_kernel(ctx_ref, up_ref, down_ref, packed_ref):
    share, units = up_ref.shape
    for half in range(2):

        @pl.when(ctx_ref[0] == half)
        def _():
            lanes = slice(half * (units // 2), (half + 1) * (units // 2))
            for copy in range(packed_ref.shape[0]):
                packed_ref[copy, :share, :] = up_ref[:, lanes]
                packed_ref[copy, share:, :] = down_ref[:, lanes]


def rows_at(index, size):
    return pl.ds(pl.multiple_of(index * size, size), size)


def split_kernel(
    high_ref, ctx_ref, kept_ref, got_ref, mixed_kept_ref, mixed_away_ref, grad_kept_ref, grad_away_ref
):
    size = kept_ref.shape[1] // 4
    high, ctx = high_ref[0], ctx_ref[0]

    def total(which, c, h):
        rows = rows_at(c * 2 + h, size)
        both = kept_ref[which, rows, :].astype(f32) + got_ref[which, rows, :].astype(f32)
        return both.astype(bf16)

    for i in range(2):
        rows = slice(i * size, (i + 1) * size)
        mixed_kept_ref[rows, :] = total(0, i, high)
        mixed_away_ref[rows, :] = total(0, i, 1 - high)
        grad_kept_ref[rows, :] = total(1, ctx, i)
        grad_away_ref[rows, :] = total(1, 1 - ctx, i)


def halve_kernel(bit_ref, kept_ref, got_ref, kept_out_ref, away_out_ref):
    size = kept_ref.shape[0] // 2

    def total(half):
        rows = rows_at(half, size)
        return kept_ref[rows, :].astype(f32) + got_ref[rows, :].astype(f32)

    kept_out_ref[...] = total(bit_ref[0])
    away_out_ref[...] = total(1 - bit_ref[0]).astype(bf16)


def attention_kernel(shares, ctx_ref, dp_ref, *refs):
    piece_refs, refs = refs[:shares], refs[shares:]
    normed_ref, cot_ref, cos_ref, sin_ref, seg_row_ref = refs[:5]
    refs = refs[5:]
    vectors_ref, mixed_ref, grad_normed_ref, sums_ref, bias_grad_ref = refs[:5]
    part_refs, refs = refs[5 : 5 + shares], refs[5 + shares :]
    (
        weights_ref, small_ref, first_ref, qkv_ref, grad_ref, feature_ref, grad_weights_ref,
        dq_ref, dk_ref, dv_ref, seg_col_ref,
    ) = refs
    tokens, model = normed_ref.shape
    share = piece_refs[0].shape[0] - 8
    width = grad_ref.shape[0]
    scale = HD**-0.5
    ctx, dp = ctx_ref[0], dp_ref[0]
    for d, ref in enumerate(piece_refs):
        source = lax.rem(dp + (shares - d), shares)
        weights_ref[rows_at(source, share), :] = ref[:share, :]
        small_ref[source] = ref[share:, :].astype(f32)
    small = [small_ref[i] for i in range(shares)]
    vectors = jnp.concatenate([piece[:, :share] for piece in small], axis=1)
    vectors_ref[...] = vectors
    bias = sum(piece[7:8, : 3 * width] for piece in small)
    gain, shift = vectors[0:1], vectors[1:2]
    project = weights_ref[:, : 3 * width]
    output = weights_ref[:, 3 * width :]
    chunks = [slice(i, i + ROWS) for i in range(0, tokens, ROWS)]
    for rows in chunks:
        first = (normed_ref[rows, :] * gain + shift).astype(bf16)
        first_ref[rows, :] = first
        qkv_ref[:, rows] = (dot(first, project, ((1,), (0,))) + bias).T
        grad_ref[:, rows] = dot(cot_ref[rows, :], output, ((1,), (0,))).astype(bf16).T
    seg_col_ref[...] = jnp.broadcast_to(seg_row_ref[...], (8, tokens)).T
    cosine = cos_ref[...]
    sine = sin_ref[...]
    ones = jnp.ones((8, tokens), bf16)

    def rotate(block, direction):
        first, second = block[:HALF], block[HALF:ROT]
        return jnp.concatenate(
            [
                first * cosine - second * (direction * sine),
                second * cosine + first * (direction * sine),
                block[ROT:],
            ],
            axis=0,
        )

    def head(index, carry):
        start = pl.multiple_of(index * HD, HD)

        def rows(part):
            return pl.ds(part * width + start, HD)

        queries = rotate(qkv_ref[rows(0), :], 1.0).astype(bf16)
        keys = rotate(qkv_ref[rows(1), :], 1.0).astype(bf16)
        values = qkv_ref[rows(2), :].astype(bf16)
        queries = queries * jnp.asarray(scale, bf16)
        grads = grad_ref[pl.ds(start, HD), :]
        key_rows = keys.T
        value_rows = values.T
        dk_ref[...] = jnp.zeros(dk_ref.shape, f32)
        dv_ref[...] = jnp.zeros(dv_ref.shape, f32)
        for block in range(tokens // ROWS):
            begin, end = block * ROWS, (block + 1) * ROWS
            low = max(0, (begin - DOC_MAX + 1) // ROWS * ROWS)
            query = queries[:, begin:end]
            grad = grads[:, begin:end]
            scores = dot(key_rows[low:end], query, ((1,), (0,)))
            key_at = lax.broadcasted_iota(jnp.int32, scores.shape, 0) + low
            query_at = lax.broadcasted_iota(jnp.int32, scores.shape, 1) + begin
            allowed = (seg_col_ref[low:end, 0:1] == seg_row_ref[:, begin:end]) & (
                key_at <= query_at
            )
            scores = jnp.where(allowed, scores, masked_score)
            highest = jnp.max(scores, axis=0, keepdims=True)
            exponent = jnp.exp(scores - highest)
            probs = exponent * (1.0 / jnp.sum(exponent, axis=0, keepdims=True))
            probs_b = probs.astype(bf16)
            attended = dot(values[:, low:end], probs_b, ((1,), (0,))).astype(bf16)
            feature_ref[rows(3), begin:end] = attended
            delta = jnp.sum(
                grad.astype(f32) * attended.astype(f32), axis=0, keepdims=True
            )
            grad_probs = dot(value_rows[low:end], grad, ((1,), (0,)))
            grad_scores = (probs * (grad_probs - delta)).astype(bf16)
            dq_ref[:, begin:end] = dot(keys[:, low:end], grad_scores, ((1,), (0,))) * scale
            dk_ref[:, low:end] += dot(query, grad_scores, ((1,), (1,)))
            dv_ref[:, low:end] += dot(grad, probs_b, ((1,), (1,)))
        for part, result in enumerate(
            (rotate(dq_ref[...], -1.0), rotate(dk_ref[...], -1.0), dv_ref[...])
        ):
            high = result.astype(bf16)
            feature_ref[rows(part), :] = high
            rest = (result - high.astype(f32)).astype(bf16)
            total = dot(ones, high, ((1,), (1,))) + dot(ones, rest, ((1,), (1,)))
            bias_grad_ref[pl.ds(part * (width // HD) + index, 1), :] = total[0:1]
        return carry

    bias_grad_ref[...] = jnp.zeros(bias_grad_ref.shape, f32)
    lax.fori_loop(0, width // HD, head, 0)

    begin = pl.multiple_of(ctx * (2 * width), 2 * width)
    part_one = dot(feature_ref[pl.ds(begin, width), :], first_ref[...], ((1,), (0,)))
    grad_weights_ref[:, :width] = part_one.astype(bf16).T

    @pl.when(ctx == 0)
    def _():
        keys_part = dot(feature_ref[width : 2 * width, :], first_ref[...], ((1,), (0,)))
        grad_weights_ref[:, width:] = keys_part.astype(bf16).T

    @pl.when(ctx != 0)
    def _():
        output_part = dot(feature_ref[3 * width :, :], cot_ref[...], ((1,), (0,)))
        grad_weights_ref[:, width:] = output_part.astype(bf16).T

    for d, ref in enumerate(part_refs):
        ref[...] = grad_weights_ref[rows_at(lax.rem(dp + d, shares), share), :]

    total_one = jnp.zeros((1, model), f32)
    total_two = jnp.zeros((1, model), f32)
    for rows in chunks:
        attended = feature_ref[3 * width :, rows].T
        mixed_ref[rows, :] = (0.5 * dot(attended, output, ((1,), (1,)))).astype(bf16)
        grad_first = 0.5 * dot(feature_ref[: 3 * width, rows].T, project, ((1,), (1,)))
        total_one += jnp.sum(grad_first * normed_ref[rows, :], axis=0, keepdims=True)
        total_two += jnp.sum(grad_first, axis=0, keepdims=True)
        grad_normed_ref[rows, :] = (grad_first * gain).astype(bf16)
    sums_ref[0:1, :] = total_one
    sums_ref[1:2, :] = total_two


def feed_kernel(
    ctx_ref, low_ref, all_ref, normed_ref, cot_ref, vectors_ref, mixed_in_ref, grad_in_ref,
    sums_in_ref, bias_in_ref, kept_ref, away_ref, grad_weights_ref, sums_ref,
    up_ref, down_ref, second_ref, act_ref, pre_ref,
):
    tokens, model = normed_ref.shape
    shares, share, units = all_ref.shape[0], all_ref.shape[1] // 2, all_ref.shape[2]
    for s in range(shares):
        up_ref[s * share : (s + 1) * share, :] = all_ref[s, :share, :]
        down_ref[s * share : (s + 1) * share, :] = all_ref[s, share:, :]
    gain, shift = vectors_ref[2:3, :], vectors_ref[3:4, :]
    bias = jnp.where(
        ctx_ref[0] > 0, vectors_ref[6:7, units : 2 * units], vectors_ref[6:7, :units]
    )
    up, down = up_ref[...], down_ref[...]
    low = low_ref[0] > 0

    def divide(which, start, block):
        first, last = block[: ROWS // 2], block[ROWS // 2 :]
        rows = slice(start // 2, start // 2 + ROWS // 2)
        kept_ref[which, rows, :] = jnp.where(low, last, first)
        away_ref[which, rows, :] = jnp.where(low, first, last)

    total_one = jnp.zeros((1, model), f32)
    total_two = jnp.zeros((1, model), f32)
    total_bias = jnp.zeros((1, units), f32)
    total_cot = jnp.zeros((1, model), f32)
    for i in range(0, tokens, ROWS):
        rows = slice(i, i + ROWS)
        second = (normed_ref[rows, :] * gain + shift).astype(bf16)
        second_ref[rows, :] = second
        preact = dot(second, up, ((1,), (0,))) + bias
        activated, slope = gelu_pair(preact)
        act = activated.astype(bf16)
        act_ref[:, rows] = act.T
        grad_pre = dot(cot_ref[rows, :], down, ((1,), (0,))) * slope
        total_bias += jnp.sum(grad_pre, axis=0, keepdims=True)
        total_cot += jnp.sum(cot_ref[rows, :].astype(f32), axis=0, keepdims=True)
        pre = grad_pre.astype(bf16)
        pre_ref[:, rows] = pre.T
        mixed = dot(act, down, ((1,), (1,))) + mixed_in_ref[rows, :].astype(f32)
        divide(0, i, mixed.astype(bf16))
        grad_second = dot(pre, up, ((1,), (1,)))
        total_one += jnp.sum(grad_second * normed_ref[rows, :], axis=0, keepdims=True)
        total_two += jnp.sum(grad_second, axis=0, keepdims=True)
        grad_normed = grad_second * gain + grad_in_ref[rows, :].astype(f32)
        divide(1, i, grad_normed.astype(bf16))
    total_cot = 0.125 * total_cot
    up_part = dot(pre_ref[...], second_ref[...], ((1,), (0,))).astype(bf16).T
    down_part = dot(act_ref[...], cot_ref[...], ((1,), (0,))).astype(bf16).T
    for s in range(shares):
        lanes = slice(s * share, (s + 1) * share)
        grad_weights_ref[s, :share, :] = up_part[lanes]
        grad_weights_ref[s, share : 2 * share, :] = down_part[lanes]
    sums_ref[0:2, :] = sums_in_ref[...]
    sums_ref[2:3, :] = total_one
    sums_ref[3:4, :] = total_two
    sums_ref[4:5, :] = total_cot
    sums_ref[5:6, :units] = total_bias
    if shares == 1:
        return
    bias = bias_in_ref[...]
    part = HD // shares
    heads = 3 * (model // HD) // 4
    for s in range(shares):
        lanes = slice(s * share, (s + 1) * share)
        slices = [bias[i : i + 1, s * part : (s + 1) * part] for i in range(heads)]
        slices.append(jnp.zeros((1, share - heads * part), f32))
        one, two = sums_in_ref[0:1, lanes], sums_in_ref[1:2, lanes]
        values = jnp.concatenate(
            [
                jnp.concatenate([one, two], axis=1),
                jnp.concatenate([total_one[:, lanes], total_two[:, lanes]], axis=1),
                jnp.concatenate([total_cot[:, lanes]] + slices, axis=1),
                total_bias,
            ],
            axis=0,
        )
        high = values.astype(bf16)
        rest = (values - high.astype(f32)).astype(bf16)
        grad_weights_ref[s, 2 * share :, :] = jnp.concatenate(
            [high.astype(f32), rest.astype(f32)], axis=0
        ).astype(bf16)


def call(kernel, out_shape, scratch, flops, name, scalars, *args):
    whole = pl.BlockSpec(memory_space=pltpu.VMEM)
    scalar = pl.BlockSpec(memory_space=pltpu.SMEM)
    moved = sum(a.size * a.dtype.itemsize for a in args)
    return pl.pallas_call(
        kernel,
        out_shape=[jax.ShapeDtypeStruct(shape, dtype) for shape, dtype in out_shape],
        in_specs=[scalar] * len(scalars) + [whole] * len(args),
        out_specs=[whole] * len(out_shape),
        scratch_shapes=[pltpu.VMEM(shape, dtype) for shape, dtype in scratch],
        cost_estimate=pl.CostEstimate(flops=flops, transcendentals=0, bytes_accessed=moved),
        name=name,
    )(*[jnp.asarray(s, jnp.int32).reshape(1) for s in scalars], *args)


def body(
    hidden_in, cotangent, segment_ids, attend_gain, attend_shift, feed_gain, feed_shift,
    project_weight, project_bias, output_weight, output_bias,
    upward_weight, upward_bias, downward_weight, downward_bias,
):
    n_dp, n_ctx, n_tensor = (lax.axis_size(a) for a in ("dp", "ctx", "tensor"))
    dp_index, ctx_index = lax.axis_index("dp"), lax.axis_index("ctx")
    second = ctx_index > 0
    share, _, width = project_weight.shape
    model = share * n_dp
    units = upward_weight.shape[1]
    half_units = units // n_ctx
    heads = width // HD

    hidden_all = gather_tokens(hidden_in[0], True)
    columns = 4 * width
    bias_share = HD // n_dp
    tensor_index = lax.axis_index("tensor")

    (packed,) = call(
        pack_kernel, [((share + 8, columns), bf16)], [], 0, "pack_attention",
        [dp_index], project_weight.transpose(1, 0, 2), output_weight, project_bias,
        attend_gain, attend_shift, feed_gain, feed_shift, output_bias, downward_bias,
        upward_bias,
    )
    (feed_block,) = call(
        pack_feed_kernel, [((n_dp, 2 * share, half_units), bf16)], [], 0, "pack_feed",
        [ctx_index], upward_weight, downward_weight.T,
    )
    few = n_dp == 4
    if few:
        pieces = [packed] + [shifted(packed, d) for d in range(1, n_dp)]
    else:
        everything = exchange_dp(jnp.broadcast_to(packed[None], (n_dp,) + packed.shape))
        tail = everything[:, share:]
        tail = jnp.concatenate(
            [
                tail[:, :7, :share].transpose(1, 0, 2).reshape(7, model),
                jnp.sum(tail[:, 7], axis=0, keepdims=True),
            ],
            axis=0,
        )
        pieces = [
            jnp.concatenate([everything[:, :share].reshape(model, columns), tail], axis=0)
        ]
    shares = len(pieces)
    feed_block, hidden_all = lax.optimization_barrier((feed_block, hidden_all))
    feed_all = exchange_dp(feed_block)
    if not few:
        feed_all = feed_all.reshape(n_dp, 2, share, half_units).transpose(1, 0, 2, 3)
        feed_all = feed_all.reshape(1, 2 * model, half_units)

    hidden_rows = hidden_in[0]
    grad_rows = cotangent[0]
    grad_all = gather_tokens(grad_rows, False)
    tokens = hidden_all.shape[0]

    source = hidden_all.astype(f32)
    centred = source - jnp.mean(source, axis=-1, keepdims=True)
    inverse = lax.rsqrt(jnp.mean(centred * centred, axis=-1, keepdims=True) + epsilon)
    normed = centred * inverse

    frequency = 10000.0 ** (-2.0 * jnp.arange(HALF, dtype=f32) / ROT)
    angles = frequency[:, None] * jnp.arange(tokens, dtype=f32)[None, :]
    vectors, mixed, grad_normed, attention_sums, project_bias_grad, *attention_parts = call(
        functools.partial(attention_kernel, shares),
        [
            ((8, model), f32), ((tokens, model), bf16), ((tokens, model), bf16),
            ((2, model), f32), ((16, HD), f32),
        ]
        + [((model // shares, 2 * width), bf16)] * shares,
        [
            ((model, columns), bf16), ((shares, 8, columns), f32), ((tokens, model), bf16),
            ((3 * width, tokens), f32), ((width, tokens), bf16), ((columns, tokens), bf16),
            ((model, 2 * width), bf16),
            ((HD, tokens), f32), ((HD, tokens), f32), ((HD, tokens), f32),
            ((tokens, 8), jnp.int32),
        ],
        tokens * model * columns * 8,
        "attention_part",
        [ctx_index, dp_index if few else 0], *pieces, normed, grad_all,
        jnp.cos(angles), jnp.sin(angles), segment_ids,
    )
    if few:
        attention_parts = attention_parts[:1] + [
            shifted(attention_parts[d], d) for d in range(1, n_dp)
        ]
    else:
        exchanged = exchange_dp(attention_parts[0].reshape(n_dp, share, 2 * width))
        attention_parts = [exchanged[i] for i in range(n_dp)]

    kept, away, grad_feed, sums = call(
        feed_kernel,
        [
            ((2, tokens // 2, model), bf16), ((2, tokens // 2, model), bf16),
            ((shares, feed_all.shape[1] + (8 if few else 0), half_units), bf16),
            ((8, model), f32),
        ],
        [
            ((model, half_units), bf16), ((model, half_units), bf16), ((tokens, model), bf16),
            ((half_units, tokens), bf16), ((half_units, tokens), bf16),
        ],
        tokens * model * half_units * 12,
        "feed_part",
        [ctx_index, tensor_index % 2],
        feed_all, normed, grad_all, vectors, mixed, grad_normed, attention_sums,
        project_bias_grad,
    )
    kept, away, grad_feed, attention_parts = lax.optimization_barrier(
        (kept, away, grad_feed, attention_parts)
    )
    if not few:
        grad_feed = grad_feed.reshape(2, n_dp, share, half_units).transpose(1, 0, 2, 3)
        grad_feed = grad_feed.reshape(n_dp, 2 * share, half_units)
    feed_parts = exchange_dp(grad_feed)

    high_bit = tensor_index // 2
    quarter = ((tokens // 4, model), bf16)
    mixed_kept, mixed_away, grad_kept, grad_away = call(
        split_kernel, [quarter] * 4, [], 0, "split",
        [high_bit, ctx_index], kept, flipped(away, "tensor", 1),
    )
    grad_away = flipped(grad_away, "ctx", 1)
    eighths = [((tokens // 8, model), f32), ((tokens // 8, model), bf16)]
    grad_normed, grad_away = call(
        halve_kernel, eighths, [], 0, "halve_grad", [high_bit], grad_kept, grad_away
    )
    mixed, mixed_away = call(
        halve_kernel, eighths, [], 0, "halve_mixed",
        [ctx_index], mixed_kept, flipped(mixed_away, "tensor", 2),
    )
    mixed = mixed + flipped(mixed_away, "ctx", 1).astype(f32)
    grad_normed = grad_normed + flipped(grad_away, "tensor", 2).astype(f32)
    mixed, grad_normed, feed_parts = lax.optimization_barrier((mixed, grad_normed, feed_parts))
    feed_sum = jnp.sum(feed_parts.astype(f32), axis=0)

    if few:
        small = feed_sum[2 * share : 2 * share + 4] + feed_sum[2 * share + 4 :]
    else:
        bias_rows = project_bias_grad[: 3 * heads].reshape(3 * heads, n_dp, bias_share)
        bias_rows = bias_rows.transpose(1, 0, 2).reshape(n_dp, 3 * heads * bias_share)
        small = jnp.concatenate([sums[:5], sums[5:6]], axis=0)
        bit = 1
        while bit < n_dp:
            small = small + flipped(small, "dp", bit)
            bias_rows = bias_rows + flipped(bias_rows, "dp", bit)
            bit *= 2
        units_row = small[5:6, :half_units]
        small = lax.dynamic_slice_in_dim(small[:5], dp_index * share, share, 1)
        bias_row = lax.dynamic_index_in_dim(bias_rows, dp_index, 0, keepdims=False)
    if few:
        units_row = small[3:4]
        bias_row = small[2, share : share + 3 * heads * bias_share]
        small = small[:3]
    small = small + flipped(small, "tensor", 1)
    small = small + flipped(small, "tensor", 2)
    small = small + flipped(small, "ctx", 1)
    if few:
        shared = [
            small[0, :share], small[0, share:], small[1, :share], small[1, share:],
            small[2, :share],
        ]
    else:
        shared = [small[i] for i in range(5)]
    units_row = joined(units_row, flipped(units_row, "ctx", 1), second)
    upward_bias_grad = lax.dynamic_slice_in_dim(
        units_row, dp_index * (units // n_dp), units // n_dp, 1
    )
    project_bias_grad = bias_row.reshape(3, heads, bias_share)

    own_source = hidden_rows.astype(f32)
    hidden_out = own_source + mixed
    hidden_out = (hidden_out + (vectors[4] + vectors[5])).astype(bf16)[None]

    own_centred = own_source - jnp.mean(own_source, axis=-1, keepdims=True)
    own_inverse = lax.rsqrt(jnp.mean(own_centred * own_centred, axis=-1, keepdims=True) + epsilon)
    own_normed = own_centred * own_inverse
    grad_inner = own_inverse * (
        grad_normed
        - jnp.mean(grad_normed, axis=-1, keepdims=True)
        - own_normed * jnp.mean(grad_normed * own_normed, axis=-1, keepdims=True)
    )
    hidden_grad = (grad_rows.astype(f32) + grad_inner).astype(bf16)[None]

    attention_sum = sum(part.astype(f32) for part in attention_parts)
    attention_own = lax.reduce_precision(attention_sum, 8, 7).astype(bf16)
    attention_both = joined(attention_own, flipped(attention_own, "ctx", 1), second).astype(f32)

    feed_sum = feed_sum[: 2 * share]
    feed_own = lax.reduce_precision(feed_sum, 8, 7).astype(bf16)
    feed_both = joined(feed_own, flipped(feed_own, "ctx", 1), second).astype(f32)

    return (
        hidden_out,
        hidden_grad,
        shared[0],
        shared[1],
        shared[2],
        shared[3],
        attention_both[:, : 3 * width].reshape(share, 3, width),
        project_bias_grad,
        attention_both[:, 3 * width :].T,
        shared[4],
        feed_both[:share],
        upward_bias_grad,
        feed_both[share:].T,
        shared[4],
    )


def solution(mesh):
    rows = P("dp", ("ctx", "tensor"), None)
    in_specs = (
        rows, rows, P("dp", None), P("dp"), P("dp"), P("dp"), P("dp"),
        P("dp", None, "tensor"), P(None, "tensor", "dp"), P("tensor", "dp"), P("dp"),
        P("dp", "tensor"), P("tensor", "dp"), P("tensor", "dp"), P("dp"),
    )
    out_specs = (
        rows, rows, P("dp"), P("dp"), P("dp"), P("dp"),
        P("dp", None, "tensor"), P(None, "tensor", "dp"), P("tensor", "dp"), P("dp"),
        P("dp", "tensor"), P("tensor", "dp"), P("tensor", "dp"), P("dp"),
    )
    return jax.shard_map(body, mesh=mesh, in_specs=in_specs, out_specs=out_specs, check_vma=False)
```

```python
import functools

import jax
import jax.numpy as jnp
from jax import lax
from jax.experimental import pallas as pl
from jax.experimental.pallas import tpu as pltpu
from jax.sharding import PartitionSpec as P

HD = 64
ROT = 16
HALF = ROT // 2
DOC_MAX = 512
ROWS = 256

epsilon = 1e-05
masked_score = -1e30
f32 = jnp.float32
bf16 = jnp.bfloat16


def flipped(block, axis, bit):
    return lax.ppermute(block, axis, [(i, i ^ bit) for i in range(lax.axis_size(axis))])


def ordered(own, other, second, dim):
    return jnp.where(
        second, jnp.stack([other, own], axis=dim), jnp.stack([own, other], axis=dim)
    )


def joined(own, other, second):
    return jnp.where(
        second, jnp.concatenate([other, own], axis=1), jnp.concatenate([own, other], axis=1)
    )


def gather_tokens(rows, ctx_first):
    steps = [("ctx", 1, 0), ("tensor", 2, 1)] if ctx_first else [("tensor", 2, 0), ("ctx", 1, 0)]
    block = rows
    for axis, bit, dim in steps + [("tensor", 1, 2)]:
        upper = (lax.axis_index(axis) & bit) > 0
        block = ordered(block, flipped(block, axis, bit), upper, dim)
    return block.reshape(-1, rows.shape[-1])


def shifted(block, distance):
    count = lax.axis_size("dp")
    return lax.ppermute(block, "dp", [(i, (i + distance) % count) for i in range(count)])


def exchange_dp(blocks):
    return lax.all_to_all(blocks, "dp", 0, 0)


def gelu_pair(preact):
    cumulative = 0.5 * (1.0 + jax.scipy.special.erf(preact * 0.7071067811865476))
    density = jnp.exp(-0.5 * preact * preact) * 0.3989422804014327
    return (preact * cumulative, cumulative + preact * density)


def dot(left, right, dims):
    return lax.dot_general(left, right, (dims, ((), ())), preferred_element_type=f32)


def pack_kernel(dp_ref, project_ref, output_ref, bias_ref, *refs):
    vector_refs, packed_ref = refs[:-1], refs[-1]
    _, share, width = project_ref.shape
    _, heads, part = bias_ref.shape
    for i in range(3):
        packed_ref[:share, i * width : (i + 1) * width] = project_ref[i]
    packed_ref[:share, 3 * width :] = output_ref[...].T
    rest = jnp.zeros((1, 4 * width - share), f32)
    rows = [
        jnp.concatenate([ref[...].astype(f32).reshape(1, share), rest], axis=1)
        for ref in vector_refs
    ]
    lane = lax.broadcasted_iota(jnp.int32, (1, HD), 1)
    own = (lane >= dp_ref[0] * part) & (lane < (dp_ref[0] + 1) * part)
    pieces = []
    for kind in range(3):
        for head in range(heads):
            piece = bias_ref[kind, head : head + 1, :].astype(f32)
            pieces.append(jnp.where(own, jnp.concatenate([piece] * (HD // part), axis=1), 0.0))
    rows.append(jnp.concatenate(pieces + [jnp.zeros((1, width), f32)], axis=1))
    packed_ref[share:, :] = jnp.concatenate(rows, axis=0).astype(bf16)


def pack_feed_kernel(ctx_ref, up_ref, down_ref, packed_ref):
    share, units = up_ref.shape
    for half in range(2):

        @pl.when(ctx_ref[0] == half)
        def _():
            lanes = slice(half * (units // 2), (half + 1) * (units // 2))
            for copy in range(packed_ref.shape[0]):
                packed_ref[copy, :share, :] = up_ref[:, lanes]
                packed_ref[copy, share:, :] = down_ref[:, lanes]


def rows_at(index, size):
    return pl.ds(pl.multiple_of(index * size, size), size)


def split_kernel(
    high_ref, ctx_ref, kept_ref, got_ref, mixed_kept_ref, mixed_away_ref, grad_kept_ref, grad_away_ref
):
    size = kept_ref.shape[1] // 4
    high, ctx = high_ref[0], ctx_ref[0]

    def total(which, c, h):
        rows = rows_at(c * 2 + h, size)
        both = kept_ref[which, rows, :].astype(f32) + got_ref[which, rows, :].astype(f32)
        return both.astype(bf16)

    for i in range(2):
        rows = slice(i * size, (i + 1) * size)
        mixed_kept_ref[rows, :] = total(0, i, high)
        mixed_away_ref[rows, :] = total(0, i, 1 - high)
        grad_kept_ref[rows, :] = total(1, ctx, i)
        grad_away_ref[rows, :] = total(1, 1 - ctx, i)


def halve_kernel(bit_ref, kept_ref, got_ref, kept_out_ref, away_out_ref):
    size = kept_ref.shape[0] // 2

    def total(half):
        rows = rows_at(half, size)
        return kept_ref[rows, :].astype(f32) + got_ref[rows, :].astype(f32)

    kept_out_ref[...] = total(bit_ref[0])
    away_out_ref[...] = total(1 - bit_ref[0]).astype(bf16)


def attention_kernel(shares, ctx_ref, dp_ref, *refs):
    piece_refs, refs = refs[:shares], refs[shares:]
    normed_ref, cot_ref, cos_ref, sin_ref, seg_row_ref = refs[:5]
    refs = refs[5:]
    vectors_ref, weights_ref, feature_ref, bias_grad_ref = refs[:4]
    part_refs, refs = refs[4 : 4 + shares], refs[4 + shares :]
    (
        small_ref, first_ref, qkv_ref, grad_ref, grad_weights_ref, dq_ref, dk_ref, dv_ref, seg_col_ref,
    ) = refs
    tokens, model = normed_ref.shape
    share = piece_refs[0].shape[0] - 8
    width = grad_ref.shape[0]
    scale = HD**-0.5
    ctx, dp = ctx_ref[0], dp_ref[0]
    for d, ref in enumerate(piece_refs):
        source = lax.rem(dp + (shares - d), shares)
        weights_ref[rows_at(source, share), :] = ref[:share, :]
        small_ref[source] = ref[share:, :].astype(f32)
    small = [small_ref[i] for i in range(shares)]
    vectors = jnp.concatenate([piece[:, :share] for piece in small], axis=1)
    vectors_ref[...] = vectors
    bias = sum(piece[7:8, : 3 * width] for piece in small)
    gain, shift = vectors[0:1], vectors[1:2]
    project = weights_ref[:, : 3 * width]
    output = weights_ref[:, 3 * width :]
    chunks = [slice(i, i + ROWS) for i in range(0, tokens, ROWS)]
    for rows in chunks:
        first = (normed_ref[rows, :] * gain + shift).astype(bf16)
        first_ref[rows, :] = first
        qkv_ref[:, rows] = (dot(first, project, ((1,), (0,))) + bias).T
        grad_ref[:, rows] = dot(cot_ref[rows, :], output, ((1,), (0,))).astype(bf16).T
    seg_col_ref[...] = jnp.broadcast_to(seg_row_ref[...], (8, tokens)).T
    cosine = cos_ref[...]
    sine = sin_ref[...]
    ones = jnp.ones((8, tokens), bf16)

    def rotate(block, direction):
        first, second = block[:HALF], block[HALF:ROT]
        return jnp.concatenate(
            [
                first * cosine - second * (direction * sine),
                second * cosine + first * (direction * sine),
                block[ROT:],
            ],
            axis=0,
        )

    def head(index, carry):
        start = pl.multiple_of(index * HD, HD)

        def rows(part):
            return pl.ds(part * width + start, HD)

        queries = rotate(qkv_ref[rows(0), :], 1.0).astype(bf16)
        keys = rotate(qkv_ref[rows(1), :], 1.0).astype(bf16)
        values = qkv_ref[rows(2), :].astype(bf16)
        queries = queries * jnp.asarray(scale, bf16)
        grads = grad_ref[pl.ds(start, HD), :]
        key_rows = keys.T
        value_rows = values.T
        dk_ref[...] = jnp.zeros(dk_ref.shape, f32)
        dv_ref[...] = jnp.zeros(dv_ref.shape, f32)
        for block in range(tokens // ROWS):
            begin, end = block * ROWS, (block + 1) * ROWS
            low = max(0, (begin - DOC_MAX + 1) // ROWS * ROWS)
            query = queries[:, begin:end]
            grad = grads[:, begin:end]
            scores = dot(key_rows[low:end], query, ((1,), (0,)))
            key_at = lax.broadcasted_iota(jnp.int32, scores.shape, 0) + low
            query_at = lax.broadcasted_iota(jnp.int32, scores.shape, 1) + begin
            allowed = (seg_col_ref[low:end, 0:1] == seg_row_ref[:, begin:end]) & (
                key_at <= query_at
            )
            scores = jnp.where(allowed, scores, masked_score)
            highest = jnp.max(scores, axis=0, keepdims=True)
            exponent = jnp.exp(scores - highest)
            probs = exponent * (1.0 / jnp.sum(exponent, axis=0, keepdims=True))
            probs_b = probs.astype(bf16)
            attended = dot(values[:, low:end], probs_b, ((1,), (0,))).astype(bf16)
            feature_ref[rows(3), begin:end] = attended
            delta = jnp.sum(
                grad.astype(f32) * attended.astype(f32), axis=0, keepdims=True
            )
            grad_probs = dot(value_rows[low:end], grad, ((1,), (0,)))
            grad_scores = (probs * (grad_probs - delta)).astype(bf16)
            dq_ref[:, begin:end] = dot(keys[:, low:end], grad_scores, ((1,), (0,))) * scale
            dk_ref[:, low:end] += dot(query, grad_scores, ((1,), (1,)))
            dv_ref[:, low:end] += dot(grad, probs_b, ((1,), (1,)))
        for part, result in enumerate(
            (rotate(dq_ref[...], -1.0), rotate(dk_ref[...], -1.0), dv_ref[...])
        ):
            high = result.astype(bf16)
            feature_ref[rows(part), :] = high
            rest = (result - high.astype(f32)).astype(bf16)
            total = dot(ones, high, ((1,), (1,))) + dot(ones, rest, ((1,), (1,)))
            bias_grad_ref[pl.ds(part * (width // HD) + index, 1), :] = total[0:1]
        return carry

    bias_grad_ref[...] = jnp.zeros(bias_grad_ref.shape, f32)
    lax.fori_loop(0, width // HD, head, 0)

    begin = pl.multiple_of(ctx * (2 * width), 2 * width)
    part_one = dot(feature_ref[pl.ds(begin, width), :], first_ref[...], ((1,), (0,)))
    grad_weights_ref[:, :width] = part_one.astype(bf16).T

    @pl.when(ctx == 0)
    def _():
        keys_part = dot(feature_ref[width : 2 * width, :], first_ref[...], ((1,), (0,)))
        grad_weights_ref[:, width:] = keys_part.astype(bf16).T

    @pl.when(ctx != 0)
    def _():
        output_part = dot(feature_ref[3 * width :, :], cot_ref[...], ((1,), (0,)))
        grad_weights_ref[:, width:] = output_part.astype(bf16).T

    for d, ref in enumerate(part_refs):
        ref[...] = grad_weights_ref[rows_at(lax.rem(dp + d, shares), share), :]


def feed_kernel(
    ctx_ref, low_ref, all_ref, normed_ref, cot_ref, vectors_ref, weights_ref, feature_ref,
    bias_in_ref, kept_ref, away_ref, grad_weights_ref, sums_ref,
    up_ref, down_ref, second_ref, act_ref, pre_ref, mixed_in_ref, grad_in_ref, sums_in_ref,
):
    tokens, model = normed_ref.shape
    shares, share, units = all_ref.shape[0], all_ref.shape[1] // 2, all_ref.shape[2]
    for s in range(shares):
        up_ref[s * share : (s + 1) * share, :] = all_ref[s, :share, :]
        down_ref[s * share : (s + 1) * share, :] = all_ref[s, share:, :]
    width = HD * (model // HD) // 4
    project = weights_ref[:, : 3 * width]
    output = weights_ref[:, 3 * width :]
    chunks = [slice(i, i + ROWS) for i in range(0, tokens, ROWS)]
    for half in range(2):
        own = chunks[half * (len(chunks) // 2) : (half + 1) * (len(chunks) // 2)]

        @pl.when(ctx_ref[0] == half)
        def _():
            total_one = jnp.zeros((1, model), f32)
            total_two = jnp.zeros((1, model), f32)
            for rows in own:
                attended = feature_ref[3 * width :, rows].T
                mixed_in_ref[rows, :] = dot(attended, output, ((1,), (1,))).astype(bf16)
                grad_first = dot(feature_ref[: 3 * width, rows].T, project, ((1,), (1,)))
                total_one += jnp.sum(grad_first * normed_ref[rows, :], axis=0, keepdims=True)
                total_two += jnp.sum(grad_first, axis=0, keepdims=True)
                grad_in_ref[rows, :] = (grad_first * vectors_ref[0:1, :]).astype(bf16)
            sums_in_ref[0:1, :] = total_one
            sums_in_ref[1:2, :] = total_two

        @pl.when(ctx_ref[0] != half)
        def _():
            for rows in own:
                mixed_in_ref[rows, :] = jnp.zeros((ROWS, model), bf16)
                grad_in_ref[rows, :] = jnp.zeros((ROWS, model), bf16)

    gain, shift = vectors_ref[2:3, :], vectors_ref[3:4, :]
    bias = jnp.where(
        ctx_ref[0] > 0, vectors_ref[6:7, units : 2 * units], vectors_ref[6:7, :units]
    )
    up, down = up_ref[...], down_ref[...]
    low = low_ref[0] > 0

    def divide(which, start, block):
        first, last = block[: ROWS // 2], block[ROWS // 2 :]
        rows = slice(start // 2, start // 2 + ROWS // 2)
        kept_ref[which, rows, :] = jnp.where(low, last, first)
        away_ref[which, rows, :] = jnp.where(low, first, last)

    total_one = jnp.zeros((1, model), f32)
    total_two = jnp.zeros((1, model), f32)
    total_bias = jnp.zeros((1, units), f32)
    total_cot = jnp.zeros((1, model), f32)
    for i in range(0, tokens, ROWS):
        rows = slice(i, i + ROWS)
        second = (normed_ref[rows, :] * gain + shift).astype(bf16)
        second_ref[rows, :] = second
        preact = dot(second, up, ((1,), (0,))) + bias
        activated, slope = gelu_pair(preact)
        act = activated.astype(bf16)
        act_ref[:, rows] = act.T
        grad_pre = dot(cot_ref[rows, :], down, ((1,), (0,))) * slope
        total_bias += jnp.sum(grad_pre, axis=0, keepdims=True)
        total_cot += jnp.sum(cot_ref[rows, :].astype(f32), axis=0, keepdims=True)
        pre = grad_pre.astype(bf16)
        pre_ref[:, rows] = pre.T
        mixed = dot(act, down, ((1,), (1,))) + mixed_in_ref[rows, :].astype(f32)
        divide(0, i, mixed.astype(bf16))
        grad_second = dot(pre, up, ((1,), (1,)))
        total_one += jnp.sum(grad_second * normed_ref[rows, :], axis=0, keepdims=True)
        total_two += jnp.sum(grad_second, axis=0, keepdims=True)
        grad_normed = grad_second * gain + grad_in_ref[rows, :].astype(f32)
        divide(1, i, grad_normed.astype(bf16))
    total_cot = 0.125 * total_cot
    up_part = dot(pre_ref[...], second_ref[...], ((1,), (0,))).astype(bf16).T
    down_part = dot(act_ref[...], cot_ref[...], ((1,), (0,))).astype(bf16).T
    for s in range(shares):
        lanes = slice(s * share, (s + 1) * share)
        grad_weights_ref[s, :share, :] = up_part[lanes]
        grad_weights_ref[s, share : 2 * share, :] = down_part[lanes]
    sums_ref[0:2, :] = sums_in_ref[...]
    sums_ref[2:3, :] = total_one
    sums_ref[3:4, :] = total_two
    sums_ref[4:5, :] = total_cot
    sums_ref[5:6, :units] = total_bias
    if shares == 1:
        return
    bias = bias_in_ref[...]
    part = HD // shares
    heads = 3 * (model // HD) // 4
    for s in range(shares):
        lanes = slice(s * share, (s + 1) * share)
        slices = [bias[i : i + 1, s * part : (s + 1) * part] for i in range(heads)]
        slices.append(jnp.zeros((1, share - heads * part), f32))
        one, two = sums_in_ref[0:1, lanes], sums_in_ref[1:2, lanes]
        values = jnp.concatenate(
            [
                jnp.concatenate([one, two], axis=1),
                jnp.concatenate([total_one[:, lanes], total_two[:, lanes]], axis=1),
                jnp.concatenate([total_cot[:, lanes]] + slices, axis=1),
                total_bias,
            ],
            axis=0,
        )
        high = values.astype(bf16)
        rest = (values - high.astype(f32)).astype(bf16)
        grad_weights_ref[s, 2 * share :, :] = jnp.concatenate(
            [high.astype(f32), rest.astype(f32)], axis=0
        ).astype(bf16)


def call(kernel, out_shape, scratch, flops, name, scalars, *args):
    whole = pl.BlockSpec(memory_space=pltpu.VMEM)
    scalar = pl.BlockSpec(memory_space=pltpu.SMEM)
    moved = sum(a.size * a.dtype.itemsize for a in args)
    return pl.pallas_call(
        kernel,
        out_shape=[jax.ShapeDtypeStruct(shape, dtype) for shape, dtype in out_shape],
        in_specs=[scalar] * len(scalars) + [whole] * len(args),
        out_specs=[whole] * len(out_shape),
        scratch_shapes=[pltpu.VMEM(shape, dtype) for shape, dtype in scratch],
        cost_estimate=pl.CostEstimate(flops=flops, transcendentals=0, bytes_accessed=moved),
        name=name,
    )(*[jnp.asarray(s, jnp.int32).reshape(1) for s in scalars], *args)


def body(
    hidden_in, cotangent, segment_ids, attend_gain, attend_shift, feed_gain, feed_shift,
    project_weight, project_bias, output_weight, output_bias,
    upward_weight, upward_bias, downward_weight, downward_bias,
):
    n_dp, n_ctx, n_tensor = (lax.axis_size(a) for a in ("dp", "ctx", "tensor"))
    dp_index, ctx_index = lax.axis_index("dp"), lax.axis_index("ctx")
    second = ctx_index > 0
    share, _, width = project_weight.shape
    model = share * n_dp
    units = upward_weight.shape[1]
    half_units = units // n_ctx
    heads = width // HD

    hidden_all = gather_tokens(hidden_in[0], True)
    columns = 4 * width
    bias_share = HD // n_dp
    tensor_index = lax.axis_index("tensor")

    (packed,) = call(
        pack_kernel, [((share + 8, columns), bf16)], [], 0, "pack_attention",
        [dp_index], project_weight.transpose(1, 0, 2), output_weight, project_bias,
        attend_gain, attend_shift, feed_gain, feed_shift, output_bias, downward_bias,
        upward_bias,
    )
    (feed_block,) = call(
        pack_feed_kernel, [((n_dp, 2 * share, half_units), bf16)], [], 0, "pack_feed",
        [ctx_index], upward_weight, downward_weight.T,
    )
    few = n_dp == 4
    if few:
        near, far = shifted(packed, 1), shifted(packed, 3)
        near, far = lax.optimization_barrier((near, far))
        pieces = [packed, near, shifted(near, 1), far]
    else:
        everything = exchange_dp(jnp.broadcast_to(packed[None], (n_dp,) + packed.shape))
        tail = everything[:, share:]
        tail = jnp.concatenate(
            [
                tail[:, :7, :share].transpose(1, 0, 2).reshape(7, model),
                jnp.sum(tail[:, 7], axis=0, keepdims=True),
            ],
            axis=0,
        )
        pieces = [
            jnp.concatenate([everything[:, :share].reshape(model, columns), tail], axis=0)
        ]
    shares = len(pieces)
    feed_block, hidden_all = lax.optimization_barrier((feed_block, hidden_all))
    feed_all = exchange_dp(feed_block)
    if not few:
        feed_all = feed_all.reshape(n_dp, 2, share, half_units).transpose(1, 0, 2, 3)
        feed_all = feed_all.reshape(1, 2 * model, half_units)

    hidden_rows = hidden_in[0]
    grad_rows = cotangent[0]
    grad_all = gather_tokens(grad_rows, False)
    tokens = hidden_all.shape[0]

    source = hidden_all.astype(f32)
    centred = source - jnp.mean(source, axis=-1, keepdims=True)
    inverse = lax.rsqrt(jnp.mean(centred * centred, axis=-1, keepdims=True) + epsilon)
    normed = centred * inverse

    frequency = 10000.0 ** (-2.0 * jnp.arange(HALF, dtype=f32) / ROT)
    angles = frequency[:, None] * jnp.arange(tokens, dtype=f32)[None, :]
    vectors, weights, feature, project_bias_grad, *attention_parts = call(
        functools.partial(attention_kernel, shares),
        [
            ((8, model), f32), ((model, columns), bf16), ((columns, tokens), bf16),
            ((16, HD), f32),
        ]
        + [((model // shares, 2 * width), bf16)] * shares,
        [
            ((shares, 8, columns), f32), ((tokens, model), bf16),
            ((3 * width, tokens), f32), ((width, tokens), bf16),
            ((model, 2 * width), bf16),
            ((HD, tokens), f32), ((HD, tokens), f32), ((HD, tokens), f32),
            ((tokens, 8), jnp.int32),
        ],
        tokens * model * columns * 8,
        "attention_part",
        [ctx_index, dp_index if few else 0], *pieces, normed, grad_all,
        jnp.cos(angles), jnp.sin(angles), segment_ids,
    )
    if few:
        attention_parts = attention_parts[:1] + [
            shifted(attention_parts[d], d) for d in range(1, n_dp)
        ]
    else:
        exchanged = exchange_dp(attention_parts[0].reshape(n_dp, share, 2 * width))
        attention_parts = [exchanged[i] for i in range(n_dp)]

    kept, away, grad_feed, sums = call(
        feed_kernel,
        [
            ((2, tokens // 2, model), bf16), ((2, tokens // 2, model), bf16),
            ((shares, feed_all.shape[1] + (8 if few else 0), half_units), bf16),
            ((8, model), f32),
        ],
        [
            ((model, half_units), bf16), ((model, half_units), bf16), ((tokens, model), bf16),
            ((half_units, tokens), bf16), ((half_units, tokens), bf16),
            ((tokens, model), bf16), ((tokens, model), bf16), ((2, model), f32),
        ],
        tokens * model * half_units * 12,
        "feed_part",
        [ctx_index, tensor_index % 2],
        feed_all, normed, grad_all, vectors, weights, feature, project_bias_grad,
    )
    kept, away, grad_feed, attention_parts = lax.optimization_barrier(
        (kept, away, grad_feed, attention_parts)
    )
    if not few:
        grad_feed = grad_feed.reshape(2, n_dp, share, half_units).transpose(1, 0, 2, 3)
        grad_feed = grad_feed.reshape(n_dp, 2 * share, half_units)
    feed_parts = exchange_dp(grad_feed)

    high_bit = tensor_index // 2
    quarter = ((tokens // 4, model), bf16)
    mixed_kept, mixed_away, grad_kept, grad_away = call(
        split_kernel, [quarter] * 4, [], 0, "split",
        [high_bit, ctx_index], kept, flipped(away, "tensor", 1),
    )
    grad_away = flipped(grad_away, "ctx", 1)
    eighths = [((tokens // 8, model), f32), ((tokens // 8, model), bf16)]
    grad_normed, grad_away = call(
        halve_kernel, eighths, [], 0, "halve_grad", [high_bit], grad_kept, grad_away
    )
    mixed, mixed_away = call(
        halve_kernel, eighths, [], 0, "halve_mixed",
        [ctx_index], mixed_kept, flipped(mixed_away, "tensor", 2),
    )
    mixed = mixed + flipped(mixed_away, "ctx", 1).astype(f32)
    grad_normed = grad_normed + flipped(grad_away, "tensor", 2).astype(f32)
    mixed, grad_normed, feed_parts = lax.optimization_barrier((mixed, grad_normed, feed_parts))
    feed_sum = jnp.sum(feed_parts.astype(f32), axis=0)

    if few:
        small = feed_sum[2 * share : 2 * share + 4] + feed_sum[2 * share + 4 :]
    else:
        bias_rows = project_bias_grad[: 3 * heads].reshape(3 * heads, n_dp, bias_share)
        bias_rows = bias_rows.transpose(1, 0, 2).reshape(n_dp, 3 * heads * bias_share)
        small = jnp.concatenate([sums[:5], sums[5:6]], axis=0)
        bit = 1
        while bit < n_dp:
            small = small + flipped(small, "dp", bit)
            bias_rows = bias_rows + flipped(bias_rows, "dp", bit)
            bit *= 2
        units_row = small[5:6, :half_units]
        small = lax.dynamic_slice_in_dim(small[:5], dp_index * share, share, 1)
        bias_row = lax.dynamic_index_in_dim(bias_rows, dp_index, 0, keepdims=False)
    if few:
        units_row = small[3:4]
        bias_row = small[2, share : share + 3 * heads * bias_share]
        small = small[:3]
    small = small + flipped(small, "tensor", 1)
    small = small + flipped(small, "tensor", 2)
    if few:
        small = jnp.concatenate([small, units_row])
        small_got = flipped(small, "ctx", 1)
        units_got = small_got[3:]
    else:
        small_got = flipped(small, "ctx", 1)
        units_got = flipped(units_row, "ctx", 1)
    units_row = joined(units_row, units_got, second)
    small = small + small_got
    if few:
        shared = [
            small[0, :share], small[0, share:], small[1, :share], small[1, share:],
            small[2, :share],
        ]
    else:
        shared = [small[i] for i in range(5)]
    upward_bias_grad = lax.dynamic_slice_in_dim(
        units_row, dp_index * (units // n_dp), units // n_dp, 1
    )
    project_bias_grad = bias_row.reshape(3, heads, bias_share)

    own_source = hidden_rows.astype(f32)
    hidden_out = own_source + mixed
    hidden_out = (hidden_out + (vectors[4] + vectors[5])).astype(bf16)[None]

    own_centred = own_source - jnp.mean(own_source, axis=-1, keepdims=True)
    own_inverse = lax.rsqrt(jnp.mean(own_centred * own_centred, axis=-1, keepdims=True) + epsilon)
    own_normed = own_centred * own_inverse
    grad_inner = own_inverse * (
        grad_normed
        - jnp.mean(grad_normed, axis=-1, keepdims=True)
        - own_normed * jnp.mean(grad_normed * own_normed, axis=-1, keepdims=True)
    )
    hidden_grad = (grad_rows.astype(f32) + grad_inner).astype(bf16)[None]

    attention_sum = sum(part.astype(f32) for part in attention_parts)
    attention_own = lax.reduce_precision(attention_sum, 8, 7).astype(bf16)
    attention_both = joined(attention_own, flipped(attention_own, "ctx", 1), second).astype(f32)

    feed_sum = feed_sum[: 2 * share]
    feed_own = lax.reduce_precision(feed_sum, 8, 7).astype(bf16)
    feed_both = joined(feed_own, flipped(feed_own, "ctx", 1), second).astype(f32)

    return (
        hidden_out,
        hidden_grad,
        shared[0],
        shared[1],
        shared[2],
        shared[3],
        attention_both[:, : 3 * width].reshape(share, 3, width),
        project_bias_grad,
        attention_both[:, 3 * width :].T,
        shared[4],
        feed_both[:share],
        upward_bias_grad,
        feed_both[share:].T,
        shared[4],
    )


def solution(mesh):
    rows = P("dp", ("ctx", "tensor"), None)
    in_specs = (
        rows, rows, P("dp", None), P("dp"), P("dp"), P("dp"), P("dp"),
        P("dp", None, "tensor"), P(None, "tensor", "dp"), P("tensor", "dp"), P("dp"),
        P("dp", "tensor"), P("tensor", "dp"), P("tensor", "dp"), P("dp"),
    )
    out_specs = (
        rows, rows, P("dp"), P("dp"), P("dp"), P("dp"),
        P("dp", None, "tensor"), P(None, "tensor", "dp"), P("tensor", "dp"), P("dp"),
        P("dp", "tensor"), P("tensor", "dp"), P("tensor", "dp"), P("dp"),
    )
    return jax.shard_map(body, mesh=mesh, in_specs=in_specs, out_specs=out_specs, check_vma=False)
```

```python
import functools

import jax
import jax.numpy as jnp
from jax import lax
from jax.experimental import pallas as pl
from jax.experimental.pallas import tpu as pltpu
from jax.sharding import PartitionSpec as P

HD = 64
ROT = 16
HALF = ROT // 2
DOC_MAX = 512
ROWS = 256

epsilon = 1e-05
masked_score = -1e30
f32 = jnp.float32
bf16 = jnp.bfloat16


def flipped(block, axis, bit):
    return lax.ppermute(block, axis, [(i, i ^ bit) for i in range(lax.axis_size(axis))])


def ordered(own, other, second, dim):
    return jnp.where(
        second, jnp.stack([other, own], axis=dim), jnp.stack([own, other], axis=dim)
    )


def joined(own, other, second):
    return jnp.where(
        second, jnp.concatenate([other, own], axis=1), jnp.concatenate([own, other], axis=1)
    )


def gather_tokens(rows, ctx_first):
    steps = [("ctx", 1, 0), ("tensor", 2, 1)] if ctx_first else [("tensor", 2, 0), ("ctx", 1, 0)]
    block = rows
    for axis, bit, dim in steps + [("tensor", 1, 2)]:
        upper = (lax.axis_index(axis) & bit) > 0
        block = ordered(block, flipped(block, axis, bit), upper, dim)
    return block.reshape(-1, rows.shape[-1])


def shifted(block, distance):
    count = lax.axis_size("dp")
    return lax.ppermute(block, "dp", [(i, (i + distance) % count) for i in range(count)])


def exchange_dp(blocks):
    return lax.all_to_all(blocks, "dp", 0, 0)


def gelu_pair(preact):
    cumulative = 0.5 * (1.0 + jax.scipy.special.erf(preact * 0.7071067811865476))
    density = jnp.exp(-0.5 * preact * preact) * 0.3989422804014327
    return (preact * cumulative, cumulative + preact * density)


def dot(left, right, dims):
    return lax.dot_general(left, right, (dims, ((), ())), preferred_element_type=f32)


def pack_kernel(dp_ref, project_ref, output_ref, bias_ref, *refs):
    vector_refs, packed_ref = refs[:-1], refs[-1]
    _, share, width = project_ref.shape
    _, heads, part = bias_ref.shape
    for i in range(3):
        packed_ref[:share, i * width : (i + 1) * width] = project_ref[i]
    packed_ref[:share, 3 * width :] = output_ref[...].T
    rest = jnp.zeros((1, 4 * width - share), f32)
    rows = [
        jnp.concatenate([ref[...].astype(f32).reshape(1, share), rest], axis=1)
        for ref in vector_refs
    ]
    lane = lax.broadcasted_iota(jnp.int32, (1, HD), 1)
    own = (lane >= dp_ref[0] * part) & (lane < (dp_ref[0] + 1) * part)
    pieces = []
    for kind in range(3):
        for head in range(heads):
            piece = bias_ref[kind, head : head + 1, :].astype(f32)
            pieces.append(jnp.where(own, jnp.concatenate([piece] * (HD // part), axis=1), 0.0))
    rows.append(jnp.concatenate(pieces + [jnp.zeros((1, width), f32)], axis=1))
    packed_ref[share:, :] = jnp.concatenate(rows, axis=0).astype(bf16)


def pack_feed_kernel(ctx_ref, up_ref, down_ref, packed_ref):
    share, units = up_ref.shape
    for half in range(2):

        @pl.when(ctx_ref[0] == half)
        def _():
            lanes = slice(half * (units // 2), (half + 1) * (units // 2))
            for copy in range(packed_ref.shape[0]):
                packed_ref[copy, :share, :] = up_ref[:, lanes]
                packed_ref[copy, share:, :] = down_ref[:, lanes]


def rows_at(index, size):
    return pl.ds(pl.multiple_of(index * size, size), size)


def split_kernel(
    high_ref, ctx_ref, kept_ref, got_ref, mixed_kept_ref, mixed_away_ref, grad_kept_ref, grad_away_ref
):
    size = kept_ref.shape[1] // 4
    high, ctx = high_ref[0], ctx_ref[0]

    def total(which, c, h):
        rows = rows_at(c * 2 + h, size)
        both = kept_ref[which, rows, :].astype(f32) + got_ref[which, rows, :].astype(f32)
        return both.astype(bf16)

    for i in range(2):
        rows = slice(i * size, (i + 1) * size)
        mixed_kept_ref[rows, :] = total(0, i, high)
        mixed_away_ref[rows, :] = total(0, i, 1 - high)
        grad_kept_ref[rows, :] = total(1, ctx, i)
        grad_away_ref[rows, :] = total(1, 1 - ctx, i)


def halve_kernel(bit_ref, kept_ref, got_ref, kept_out_ref, away_out_ref):
    size = kept_ref.shape[0] // 2

    def total(half):
        rows = rows_at(half, size)
        return kept_ref[rows, :].astype(f32) + got_ref[rows, :].astype(f32)

    kept_out_ref[...] = total(bit_ref[0])
    away_out_ref[...] = total(1 - bit_ref[0]).astype(bf16)


def attention_kernel(shares, ctx_ref, dp_ref, *refs):
    piece_refs, refs = refs[:shares], refs[shares:]
    normed_ref, cot_ref, cos_ref, sin_ref, seg_row_ref = refs[:5]
    refs = refs[5:]
    vectors_ref, weights_ref, feature_ref, bias_grad_ref = refs[:4]
    part_refs, refs = refs[4 : 4 + shares], refs[4 + shares :]
    (
        small_ref, first_ref, qkv_ref, grad_ref, grad_weights_ref, dq_ref, dk_ref, dv_ref, seg_col_ref,
    ) = refs
    tokens, model = normed_ref.shape
    share = piece_refs[0].shape[0] - 8
    width = grad_ref.shape[0]
    scale = HD**-0.5
    ctx, dp = ctx_ref[0], dp_ref[0]
    for d, ref in enumerate(piece_refs):
        source = lax.rem(dp + (shares - d), shares)
        weights_ref[rows_at(source, share), :] = ref[:share, :]
        small_ref[source] = ref[share:, :].astype(f32)
    small = [small_ref[i] for i in range(shares)]
    vectors = jnp.concatenate([piece[:, :share] for piece in small], axis=1)
    vectors_ref[...] = vectors
    bias = sum(piece[7:8, : 3 * width] for piece in small)
    gain, shift = vectors[0:1], vectors[1:2]
    project = weights_ref[:, : 3 * width]
    output = weights_ref[:, 3 * width :]
    chunks = [slice(i, i + ROWS) for i in range(0, tokens, ROWS)]
    for rows in chunks:
        first = (normed_ref[rows, :] * gain + shift).astype(bf16)
        first_ref[rows, :] = first
        qkv_ref[:, rows] = (dot(first, project, ((1,), (0,))) + bias).T
        grad_ref[:, rows] = dot(cot_ref[rows, :], output, ((1,), (0,))).astype(bf16).T
    seg_col_ref[...] = jnp.broadcast_to(seg_row_ref[...], (8, tokens)).T
    cosine = cos_ref[...]
    sine = sin_ref[...]
    ones = jnp.ones((8, tokens), bf16)

    def rotate(block, direction):
        first, second = block[:HALF], block[HALF:ROT]
        return jnp.concatenate(
            [
                first * cosine - second * (direction * sine),
                second * cosine + first * (direction * sine),
                block[ROT:],
            ],
            axis=0,
        )

    def head(index, carry):
        start = pl.multiple_of(index * HD, HD)

        def rows(part):
            return pl.ds(part * width + start, HD)

        queries = rotate(qkv_ref[rows(0), :], 1.0).astype(bf16)
        keys = rotate(qkv_ref[rows(1), :], 1.0).astype(bf16)
        values = qkv_ref[rows(2), :].astype(bf16)
        queries = queries * jnp.asarray(scale, bf16)
        grads = grad_ref[pl.ds(start, HD), :]
        key_rows = keys.T
        value_rows = values.T
        dk_ref[...] = jnp.zeros(dk_ref.shape, f32)
        dv_ref[...] = jnp.zeros(dv_ref.shape, f32)
        for block in range(tokens // ROWS):
            begin, end = block * ROWS, (block + 1) * ROWS
            low = max(0, (begin - DOC_MAX + 1) // ROWS * ROWS)
            query = queries[:, begin:end]
            grad = grads[:, begin:end]
            scores = dot(key_rows[low:end], query, ((1,), (0,)))
            key_at = lax.broadcasted_iota(jnp.int32, scores.shape, 0) + low
            query_at = lax.broadcasted_iota(jnp.int32, scores.shape, 1) + begin
            allowed = (seg_col_ref[low:end, 0:1] == seg_row_ref[:, begin:end]) & (
                key_at <= query_at
            )
            scores = jnp.where(allowed, scores, masked_score)
            highest = jnp.max(scores, axis=0, keepdims=True)
            exponent = jnp.exp(scores - highest)
            probs = exponent * (1.0 / jnp.sum(exponent, axis=0, keepdims=True))
            probs_b = probs.astype(bf16)
            attended = dot(values[:, low:end], probs_b, ((1,), (0,))).astype(bf16)
            feature_ref[rows(3), begin:end] = attended
            delta = jnp.sum(
                grad.astype(f32) * attended.astype(f32), axis=0, keepdims=True
            )
            grad_probs = dot(value_rows[low:end], grad, ((1,), (0,)))
            grad_scores = (probs * (grad_probs - delta)).astype(bf16)
            dq_ref[:, begin:end] = dot(keys[:, low:end], grad_scores, ((1,), (0,))) * scale
            dk_ref[:, low:end] += dot(query, grad_scores, ((1,), (1,)))
            dv_ref[:, low:end] += dot(grad, probs_b, ((1,), (1,)))
        for part, result in enumerate(
            (rotate(dq_ref[...], -1.0), rotate(dk_ref[...], -1.0), dv_ref[...])
        ):
            high = result.astype(bf16)
            feature_ref[rows(part), :] = high
            rest = (result - high.astype(f32)).astype(bf16)
            total = dot(ones, high, ((1,), (1,))) + dot(ones, rest, ((1,), (1,)))
            bias_grad_ref[pl.ds(part * (width // HD) + index, 1), :] = total[0:1]
        return carry

    bias_grad_ref[...] = jnp.zeros(bias_grad_ref.shape, f32)
    lax.fori_loop(0, width // HD, head, 0)

    begin = pl.multiple_of(ctx * (2 * width), 2 * width)
    part_one = dot(feature_ref[pl.ds(begin, width), :], first_ref[...], ((1,), (0,)))
    grad_weights_ref[:, :width] = part_one.astype(bf16).T

    @pl.when(ctx == 0)
    def _():
        keys_part = dot(feature_ref[width : 2 * width, :], first_ref[...], ((1,), (0,)))
        grad_weights_ref[:, width:] = keys_part.astype(bf16).T

    @pl.when(ctx != 0)
    def _():
        output_part = dot(feature_ref[3 * width :, :], cot_ref[...], ((1,), (0,)))
        grad_weights_ref[:, width:] = output_part.astype(bf16).T

    for d, ref in enumerate(part_refs):
        ref[...] = grad_weights_ref[rows_at(lax.rem(dp + d, shares), share), :]


def feed_kernel(
    ctx_ref, low_ref, all_ref, normed_ref, cot_ref, vectors_ref, weights_ref, feature_ref,
    bias_in_ref, kept_ref, away_ref, grad_weights_ref, sums_ref,
    up_ref, down_ref, second_ref, act_ref, pre_ref, mixed_in_ref, grad_in_ref, sums_in_ref,
):
    tokens, model = normed_ref.shape
    shares, share, units = all_ref.shape[0], all_ref.shape[1] // 2, all_ref.shape[2]
    for s in range(shares):
        up_ref[s * share : (s + 1) * share, :] = all_ref[s, :share, :]
        down_ref[s * share : (s + 1) * share, :] = all_ref[s, share:, :]
    width = HD * (model // HD) // 4
    project = weights_ref[:, : 3 * width]
    output = weights_ref[:, 3 * width :]
    chunks = [slice(i, i + ROWS) for i in range(0, tokens, ROWS)]
    for half in range(2):
        own = chunks[half * (len(chunks) // 2) : (half + 1) * (len(chunks) // 2)]

        @pl.when(ctx_ref[0] == half)
        def _():
            total_one = jnp.zeros((1, model), f32)
            total_two = jnp.zeros((1, model), f32)
            for rows in own:
                attended = feature_ref[3 * width :, rows].T
                mixed_in_ref[rows, :] = dot(attended, output, ((1,), (1,))).astype(bf16)
                grad_first = dot(feature_ref[: 3 * width, rows].T, project, ((1,), (1,)))
                total_one += jnp.sum(grad_first * normed_ref[rows, :], axis=0, keepdims=True)
                total_two += jnp.sum(grad_first, axis=0, keepdims=True)
                grad_in_ref[rows, :] = (grad_first * vectors_ref[0:1, :]).astype(bf16)
            sums_in_ref[0:1, :] = total_one
            sums_in_ref[1:2, :] = total_two

        @pl.when(ctx_ref[0] != half)
        def _():
            for rows in own:
                mixed_in_ref[rows, :] = jnp.zeros((ROWS, model), bf16)
                grad_in_ref[rows, :] = jnp.zeros((ROWS, model), bf16)

    gain, shift = vectors_ref[2:3, :], vectors_ref[3:4, :]
    bias = jnp.where(
        ctx_ref[0] > 0, vectors_ref[6:7, units : 2 * units], vectors_ref[6:7, :units]
    )
    up, down = up_ref[...], down_ref[...]
    low = low_ref[0] > 0

    def divide(which, start, block):
        first, last = block[: ROWS // 2], block[ROWS // 2 :]
        rows = slice(start // 2, start // 2 + ROWS // 2)
        kept_ref[which, rows, :] = jnp.where(low, last, first)
        away_ref[which, rows, :] = jnp.where(low, first, last)

    total_one = jnp.zeros((1, model), f32)
    total_two = jnp.zeros((1, model), f32)
    total_bias = jnp.zeros((1, units), f32)
    total_cot = jnp.zeros((1, model), f32)
    for i in range(0, tokens, ROWS):
        rows = slice(i, i + ROWS)
        second = (normed_ref[rows, :] * gain + shift).astype(bf16)
        second_ref[rows, :] = second
        preact = dot(second, up, ((1,), (0,))) + bias
        activated, slope = gelu_pair(preact)
        act = activated.astype(bf16)
        act_ref[:, rows] = act.T
        grad_pre = dot(cot_ref[rows, :], down, ((1,), (0,))) * slope
        total_bias += jnp.sum(grad_pre, axis=0, keepdims=True)
        total_cot += jnp.sum(cot_ref[rows, :].astype(f32), axis=0, keepdims=True)
        pre = grad_pre.astype(bf16)
        pre_ref[:, rows] = pre.T
        mixed = dot(act, down, ((1,), (1,))) + mixed_in_ref[rows, :].astype(f32)
        divide(0, i, mixed.astype(bf16))
        grad_second = dot(pre, up, ((1,), (1,)))
        total_one += jnp.sum(grad_second * normed_ref[rows, :], axis=0, keepdims=True)
        total_two += jnp.sum(grad_second, axis=0, keepdims=True)
        grad_normed = grad_second * gain + grad_in_ref[rows, :].astype(f32)
        divide(1, i, grad_normed.astype(bf16))
    total_cot = 0.125 * total_cot
    up_part = dot(pre_ref[...], second_ref[...], ((1,), (0,))).astype(bf16).T
    down_part = dot(act_ref[...], cot_ref[...], ((1,), (0,))).astype(bf16).T
    for s in range(shares):
        lanes = slice(s * share, (s + 1) * share)
        grad_weights_ref[s, :share, :] = up_part[lanes]
        grad_weights_ref[s, share : 2 * share, :] = down_part[lanes]
    sums_ref[0:2, :] = sums_in_ref[...]
    sums_ref[2:3, :] = total_one
    sums_ref[3:4, :] = total_two
    sums_ref[4:5, :] = total_cot
    sums_ref[5:6, :units] = total_bias
    if shares == 1:
        return
    bias = bias_in_ref[...]
    part = HD // shares
    heads = 3 * (model // HD) // 4
    for s in range(shares):
        lanes = slice(s * share, (s + 1) * share)
        slices = [bias[i : i + 1, s * part : (s + 1) * part] for i in range(heads)]
        slices.append(jnp.zeros((1, share - heads * part), f32))
        one, two = sums_in_ref[0:1, lanes], sums_in_ref[1:2, lanes]
        values = jnp.concatenate(
            [
                jnp.concatenate([one, two], axis=1),
                jnp.concatenate([total_one[:, lanes], total_two[:, lanes]], axis=1),
                jnp.concatenate([total_cot[:, lanes]] + slices, axis=1),
                total_bias,
            ],
            axis=0,
        )
        high = values.astype(bf16)
        rest = (values - high.astype(f32)).astype(bf16)
        grad_weights_ref[s, 2 * share :, :] = jnp.concatenate(
            [high.astype(f32), rest.astype(f32)], axis=0
        ).astype(bf16)


def call(kernel, out_shape, scratch, flops, name, scalars, *args):
    whole = pl.BlockSpec(memory_space=pltpu.VMEM)
    scalar = pl.BlockSpec(memory_space=pltpu.SMEM)
    moved = sum(a.size * a.dtype.itemsize for a in args)
    return pl.pallas_call(
        kernel,
        out_shape=[jax.ShapeDtypeStruct(shape, dtype) for shape, dtype in out_shape],
        in_specs=[scalar] * len(scalars) + [whole] * len(args),
        out_specs=[whole] * len(out_shape),
        scratch_shapes=[pltpu.VMEM(shape, dtype) for shape, dtype in scratch],
        cost_estimate=pl.CostEstimate(flops=flops, transcendentals=0, bytes_accessed=moved),
        name=name,
    )(*[jnp.asarray(s, jnp.int32).reshape(1) for s in scalars], *args)


def body(
    hidden_in, cotangent, segment_ids, attend_gain, attend_shift, feed_gain, feed_shift,
    project_weight, project_bias, output_weight, output_bias,
    upward_weight, upward_bias, downward_weight, downward_bias,
):
    n_dp, n_ctx, n_tensor = (lax.axis_size(a) for a in ("dp", "ctx", "tensor"))
    dp_index, ctx_index = lax.axis_index("dp"), lax.axis_index("ctx")
    second = ctx_index > 0
    share, _, width = project_weight.shape
    model = share * n_dp
    units = upward_weight.shape[1]
    half_units = units // n_ctx
    heads = width // HD

    hidden_all = gather_tokens(hidden_in[0], True)
    columns = 4 * width
    bias_share = HD // n_dp
    tensor_index = lax.axis_index("tensor")

    (packed,) = call(
        pack_kernel, [((share + 8, columns), bf16)], [], 0, "pack_attention",
        [dp_index], project_weight.transpose(1, 0, 2), output_weight, project_bias,
        attend_gain, attend_shift, feed_gain, feed_shift, output_bias, downward_bias,
        upward_bias,
    )
    (feed_block,) = call(
        pack_feed_kernel, [((n_dp, 2 * share, half_units), bf16)], [], 0, "pack_feed",
        [ctx_index], upward_weight, downward_weight.T,
    )
    few = n_dp == 4
    if few:
        near, far = shifted(packed, 1), shifted(packed, 3)
        near, far = lax.optimization_barrier((near, far))
        pieces = [packed, near, shifted(near, 1), far]
    else:
        everything = exchange_dp(jnp.broadcast_to(packed[None], (n_dp,) + packed.shape))
        tail = everything[:, share:]
        tail = jnp.concatenate(
            [
                tail[:, :7, :share].transpose(1, 0, 2).reshape(7, model),
                jnp.sum(tail[:, 7], axis=0, keepdims=True),
            ],
            axis=0,
        )
        pieces = [
            jnp.concatenate([everything[:, :share].reshape(model, columns), tail], axis=0)
        ]
    shares = len(pieces)
    feed_block, hidden_all = lax.optimization_barrier((feed_block, hidden_all))
    feed_all = exchange_dp(feed_block)
    if not few:
        feed_all = feed_all.reshape(n_dp, 2, share, half_units).transpose(1, 0, 2, 3)
        feed_all = feed_all.reshape(1, 2 * model, half_units)

    hidden_rows = hidden_in[0]
    grad_rows = cotangent[0]
    grad_all = gather_tokens(grad_rows, False)
    tokens = hidden_all.shape[0]

    source = hidden_all.astype(f32)
    centred = source - jnp.mean(source, axis=-1, keepdims=True)
    inverse = lax.rsqrt(jnp.mean(centred * centred, axis=-1, keepdims=True) + epsilon)
    normed = centred * inverse

    frequency = 10000.0 ** (-2.0 * jnp.arange(HALF, dtype=f32) / ROT)
    angles = frequency[:, None] * jnp.arange(tokens, dtype=f32)[None, :]
    vectors, weights, feature, project_bias_grad, *attention_parts = call(
        functools.partial(attention_kernel, shares),
        [
            ((8, model), f32), ((model, columns), bf16), ((columns, tokens), bf16),
            ((16, HD), f32),
        ]
        + [((model // shares, 2 * width), bf16)] * shares,
        [
            ((shares, 8, columns), f32), ((tokens, model), bf16),
            ((3 * width, tokens), f32), ((width, tokens), bf16),
            ((model, 2 * width), bf16),
            ((HD, tokens), f32), ((HD, tokens), f32), ((HD, tokens), f32),
            ((tokens, 8), jnp.int32),
        ],
        tokens * model * columns * 8,
        "attention_part",
        [ctx_index, dp_index if few else 0], *pieces, normed, grad_all,
        jnp.cos(angles), jnp.sin(angles), segment_ids,
    )
    if few:
        attention_parts = attention_parts[:1] + [
            shifted(attention_parts[d], d) for d in range(1, n_dp)
        ]
    else:
        exchanged = exchange_dp(attention_parts[0].reshape(n_dp, share, 2 * width))
        attention_parts = [exchanged[i] for i in range(n_dp)]

    kept, away, grad_feed, sums = call(
        feed_kernel,
        [
            ((2, tokens // 2, model), bf16), ((2, tokens // 2, model), bf16),
            ((shares, feed_all.shape[1] + (8 if few else 0), half_units), bf16),
            ((8, model), f32),
        ],
        [
            ((model, half_units), bf16), ((model, half_units), bf16), ((tokens, model), bf16),
            ((half_units, tokens), bf16), ((half_units, tokens), bf16),
            ((tokens, model), bf16), ((tokens, model), bf16), ((2, model), f32),
        ],
        tokens * model * half_units * 12,
        "feed_part",
        [ctx_index, tensor_index % 2],
        feed_all, normed, grad_all, vectors, weights, feature, project_bias_grad,
    )
    kept, away, grad_feed, attention_parts = lax.optimization_barrier(
        (kept, away, grad_feed, attention_parts)
    )
    if not few:
        grad_feed = grad_feed.reshape(2, n_dp, share, half_units).transpose(1, 0, 2, 3)
        grad_feed = grad_feed.reshape(n_dp, 2 * share, half_units)
    feed_parts = exchange_dp(grad_feed)

    high_bit = tensor_index // 2
    quarter = ((tokens // 4, model), bf16)
    mixed_kept, mixed_away, grad_kept, grad_away = call(
        split_kernel, [quarter] * 4, [], 0, "split",
        [high_bit, ctx_index], kept, flipped(away, "tensor", 1),
    )
    grad_away = flipped(grad_away, "ctx", 1)
    eighths = [((tokens // 8, model), f32), ((tokens // 8, model), bf16)]
    grad_normed, grad_away = call(
        halve_kernel, eighths, [], 0, "halve_grad", [high_bit], grad_kept, grad_away
    )
    mixed, mixed_away = call(
        halve_kernel, eighths, [], 0, "halve_mixed",
        [ctx_index], mixed_kept, flipped(mixed_away, "tensor", 2),
    )
    mixed = mixed + flipped(mixed_away, "ctx", 1).astype(f32)
    grad_normed = grad_normed + flipped(grad_away, "tensor", 2).astype(f32)
    mixed, grad_normed, feed_parts = lax.optimization_barrier((mixed, grad_normed, feed_parts))
    feed_sum = jnp.sum(feed_parts.astype(f32), axis=0)

    if few:
        small = feed_sum[2 * share : 2 * share + 4] + feed_sum[2 * share + 4 :]
    else:
        bias_rows = project_bias_grad[: 3 * heads].reshape(3 * heads, n_dp, bias_share)
        bias_rows = bias_rows.transpose(1, 0, 2).reshape(n_dp, 3 * heads * bias_share)
        small = jnp.concatenate([sums[:5], sums[5:6]], axis=0)
        bit = 1
        while bit < n_dp:
            small = small + flipped(small, "dp", bit)
            bias_rows = bias_rows + flipped(bias_rows, "dp", bit)
            bit *= 2
        units_row = small[5:6, :half_units]
        small = lax.dynamic_slice_in_dim(small[:5], dp_index * share, share, 1)
        bias_row = lax.dynamic_index_in_dim(bias_rows, dp_index, 0, keepdims=False)
    if few:
        units_row = small[3:4]
        bias_row = small[2, share : share + 3 * heads * bias_share]
        small = small[:3]
    if few:
        small = jnp.concatenate([small, units_row])
        small_got = flipped(small, "ctx", 1)
        units_got = small_got[3:]
    else:
        small_got = flipped(small, "ctx", 1)
        units_got = flipped(units_row, "ctx", 1)
    units_row = joined(units_row, units_got, second)
    small = small + small_got
    small = small[:3] if few else small
    small = small + flipped(small, "tensor", 2)
    small = small + flipped(small, "tensor", 1)
    if few:
        shared = [
            small[0, :share], small[0, share:], small[1, :share], small[1, share:],
            small[2, :share],
        ]
    else:
        shared = [small[i] for i in range(5)]
    upward_bias_grad = lax.dynamic_slice_in_dim(
        units_row, dp_index * (units // n_dp), units // n_dp, 1
    )
    project_bias_grad = bias_row.reshape(3, heads, bias_share)

    own_source = hidden_rows.astype(f32)
    hidden_out = own_source + mixed
    hidden_out = (hidden_out + (vectors[4] + vectors[5])).astype(bf16)[None]

    own_centred = own_source - jnp.mean(own_source, axis=-1, keepdims=True)
    own_inverse = lax.rsqrt(jnp.mean(own_centred * own_centred, axis=-1, keepdims=True) + epsilon)
    own_normed = own_centred * own_inverse
    grad_inner = own_inverse * (
        grad_normed
        - jnp.mean(grad_normed, axis=-1, keepdims=True)
        - own_normed * jnp.mean(grad_normed * own_normed, axis=-1, keepdims=True)
    )
    hidden_grad = (grad_rows.astype(f32) + grad_inner).astype(bf16)[None]

    attention_sum = sum(part.astype(f32) for part in attention_parts)
    attention_own = lax.reduce_precision(attention_sum, 8, 7).astype(bf16)
    attention_both = joined(attention_own, flipped(attention_own, "ctx", 1), second).astype(f32)

    feed_sum = feed_sum[: 2 * share]
    feed_own = lax.reduce_precision(feed_sum, 8, 7).astype(bf16)
    feed_both = joined(feed_own, flipped(feed_own, "ctx", 1), second).astype(f32)

    return (
        hidden_out,
        hidden_grad,
        shared[0],
        shared[1],
        shared[2],
        shared[3],
        attention_both[:, : 3 * width].reshape(share, 3, width),
        project_bias_grad,
        attention_both[:, 3 * width :].T,
        shared[4],
        feed_both[:share],
        upward_bias_grad,
        feed_both[share:].T,
        shared[4],
    )


def solution(mesh):
    rows = P("dp", ("ctx", "tensor"), None)
    in_specs = (
        rows, rows, P("dp", None), P("dp"), P("dp"), P("dp"), P("dp"),
        P("dp", None, "tensor"), P(None, "tensor", "dp"), P("tensor", "dp"), P("dp"),
        P("dp", "tensor"), P("tensor", "dp"), P("tensor", "dp"), P("dp"),
    )
    out_specs = (
        rows, rows, P("dp"), P("dp"), P("dp"), P("dp"),
        P("dp", None, "tensor"), P(None, "tensor", "dp"), P("tensor", "dp"), P("dp"),
        P("dp", "tensor"), P("tensor", "dp"), P("tensor", "dp"), P("dp"),
    )
    return jax.shard_map(body, mesh=mesh, in_specs=in_specs, out_specs=out_specs, check_vma=False)
```
